256 devices in a mesh: seg: 2 (over x_hi), rad: 4 (over x_lo, core), ax: 32 (over z, y).
Axes of the slice: x: 4 (x_hi: 2, x_lo: 2; x = x_hi * 2 + x_lo), y: 4, z: 8, core: 2. Of those that a mesh axis runs over, the one named last changes fastest.
Arguments:
- start_states: float32 [4, 3, 128, 192, 384], P('seg', None, 'ax', 'rad'), may hold values from -4.2 to 4.2
- radial_inverse: float32 [192, 192, 192], P('ax'), may hold values from 0 to 1.2, as said below
- offsets: int32 [4], P('seg'), may hold values from 0 to 127
- mode_count: int32 [1], replicated, may hold values from 128 to 192
Outputs:
- residual: float32 [4, 3, 128, 192, 384], P('seg', None, 'ax', 'rad')
The draws below stay inside these ranges and needn't reach their ends.
Inputs may be any that keep to these rules, and one draw needn't show every extreme that they name: `radial_inverse`: for each mode, a dense matrix with positive entries.
All inputs are finite; a program needn't handle non-finite values.
Results may differ from the reference program's by a relative error of at most 0.0001.
Values sent between devices are 32-bit elements; how exact they have to be, the bound alone decides.
A program may use at most 128 MiB of HBM per device.

```python
import math
import jax
import jax.numpy as jnp
from jax import lax

R = 192
NM = 192
NTH = 384
NZ = 128
SEGS = 4
STEPS = 2


def draw_radial_inverse(key, part):
    length_key, factor_key = jax.random.split(key)
    lengths = jnp.exp(jax.random.uniform(length_key, (NM, 1, 1), jnp.float32, math.log(70.0), math.log(400.0)))
    factors = jax.random.uniform(factor_key, (NM, R, R), jnp.float32, 0.5, 1.5)
    positions = jnp.arange(R).astype(jnp.float32)
    distance = jnp.abs(positions[:, None] - positions[None, :])
    return jnp.eye(R, dtype=jnp.float32)[None] + 0.1 * jnp.exp(-distance[None] / lengths) * factors


def with_ends(values, stream_key, low, top_value):
    spot = [jax.random.randint(jax.random.fold_in(stream_key, axis), (), 0, length) for axis, length in enumerate(values.shape)]
    longest = values.shape.index(max(values.shape))
    next_to = spot[:longest] + [(spot[longest] + 1) % values.shape[longest]] + spot[longest + 1:]
    return values.at[tuple(spot)].set(low).at[tuple(next_to)].set(top_value)


def block_levels(rng, extent, cuts, smallest, high):
    gain, own = 1.0, jax.random.fold_in(rng, 6)
    for dim, parts in cuts:
        draws = jnp.exp(jax.random.uniform(jax.random.fold_in(own, dim), (parts,), jnp.float32, smallest / len(cuts), high / len(cuts)))
        gain = gain * jnp.repeat(draws, extent[dim] // parts).reshape([-1 if axis == dim else 1 for axis in range(len(extent))])
    return gain


def normal_values(key, dims, spread, bound, shards=(), kind=jnp.bfloat16):
    gain = block_levels(key, dims, shards, -0.22, 0.18) if shards else 1.0
    array = jax.random.normal(key, dims, jnp.float32) * spread * gain
    return jnp.minimum(jnp.maximum(array, -bound), bound).astype(kind)


def setup_inputs(seed: int = 0) -> dict:
    arg_keys = jax.random.split(jax.random.key(seed), 5)
    return {
        "start_states": normal_values(arg_keys[0], (SEGS, 3, NZ, R, NTH), 0.7, 4.2, ((0, 2), (2, 32), (3, 4)), jnp.float32),
        "radial_inverse": draw_radial_inverse(jax.random.fold_in(arg_keys[4], 71), 0),
        "offsets": with_ends(jax.random.randint(arg_keys[2], (SEGS,), 0, NZ), jax.random.fold_in(arg_keys[2], 1), 0, NZ - 1).astype(jnp.int32),
        "mode_count": jax.random.randint(arg_keys[3], (1,), NM * 2 // 3, NM + 1).astype(jnp.int32),
    }


def synthesize(coefficients):
    cosine_part = coefficients[..., 0::2]
    sine_part = coefficients[..., 1::2]
    spectrum = (cosine_part - 1j * sine_part) * (NTH / 2.0)
    spectrum = spectrum.at[..., 0].set(cosine_part[..., 0] * NTH)
    spectrum = jnp.concatenate([spectrum, jnp.zeros_like(spectrum[..., :1])], axis=-1)
    return jnp.fft.irfft(spectrum, n=NTH, axis=-1) / math.sqrt(NM)

def analyze(field, kept_modes):
    spectrum = jnp.fft.rfft(field, axis=-1)[..., :NM]
    mode_index = jnp.arange(NM)
    scale = math.sqrt(NM) / NTH
    cosine_part = jnp.real(spectrum) * jnp.where(mode_index == 0, 1.0, 2.0) * scale
    sine_part = -jnp.imag(spectrum) * (2.0 * scale)
    stacked = jnp.stack([cosine_part, sine_part], axis=-1)
    stacked = jnp.where((mode_index < kept_modes)[:, None], stacked, 0.0)
    return stacked.reshape(field.shape)

def advance(current, radial_inverse, kept_modes, profile):
    physical = synthesize(current)
    gradient = (jnp.roll(physical, -1, axis=1) - jnp.roll(physical, 1, axis=1)) * 20.0
    forcing = physical - 0.02 * (profile + physical[2:3]) * gradient
    spectral = analyze(forcing, kept_modes).reshape(3, NZ, R, NM, 2)
    solved = jnp.einsum('mrs,czsmk->czrmk', radial_inverse, spectral, precision=lax.Precision.HIGHEST)
    return solved.reshape(3, NZ, R, NTH)

def reference(start_states, radial_inverse, offsets, mode_count):
    radius = (jnp.arange(R).astype(jnp.float32) + 0.5) / R
    profile = (1.0 - radius * radius).reshape(1, 1, R, 1)
    results = []
    for segment in range(SEGS):
        current = start_states[segment]
        for step_index in range(STEPS):
            current = advance(current, radial_inverse, mode_count[0], profile)
        rolled = jnp.roll(current, offsets[segment], axis=1)
        results.append(rolled - start_states[(segment + 1) % SEGS])
    return jnp.stack(results, axis=0)
```

```python
import math

import numpy as np
import jax
import jax.numpy as jnp
from jax import lax
from jax.sharding import PartitionSpec as P

STEPS = 2


highest = lax.Precision.HIGHEST


def passed_along(value, axis, steps):
    count = lax.axis_size(axis)
    pairs = [(source, (source + steps) % count) for source in range(count)]
    return lax.ppermute(value, axis, pairs)


def padded_2(array, sides, width):
    for axis, dim in sides:
        peers, length = (lax.axis_size(axis), array.shape[dim])
        up = [(i, (i + 1) % peers) for i in range(peers)]
        down = [(j, i) for i, j in up]
        last = lax.slice_in_dim(array, length - width, length, axis=dim)
        leading = lax.slice_in_dim(array, 0, width, axis=dim)
        before = lax.ppermute(last, axis, up)
        after = lax.ppermute(leading, axis, down)
        array = jnp.concatenate([before, array, after], axis=dim)
    return array


def mode_classes(ax_count, local_modes, classes):
    assert local_modes == 6 and classes == 4 and ax_count % 2 == 0
    slots = np.array(
        [[[0, 1], [2, 3], [4, 4], [5, 5]], [[0, 0], [1, 1], [2, 3], [4, 5]]], np.int32
    )
    keep = np.array([[0, 1, 2], [0, 1, 2], [0, 2, 3], [0, 2, 3]], np.int32)
    class_modes = []
    for q in range(classes):
        modes = []
        for pair in range(ax_count // 2):
            flat = []
            for parity in range(2):
                device = 2 * pair + parity
                for slot in range(2):
                    flat.append(device * local_modes + slots[parity][q][slot])
            modes.extend(flat[u] for u in keep[q])
        class_modes.append(modes)
    class_modes = np.array(class_modes, np.int32)
    columns = np.stack([2 * class_modes, 2 * class_modes + 1], axis=-1).reshape(-1)
    return slots, keep, columns


def fourier_tables(columns, kept_modes, order):
    modes_total = columns // 2
    row_index = jnp.asarray(order)[:, None]
    point_index = lax.broadcasted_iota(jnp.int32, (columns, columns), 1)
    mode_index = row_index // 2
    phase = (mode_index * point_index % columns).astype(jnp.float32) * (2.0 * math.pi / columns)
    even_rows = row_index % 2 == 0
    cosine = jnp.cos(phase)
    sine = jnp.sin(phase)
    root = math.sqrt(modes_total)
    synthesis = jnp.where(even_rows, cosine, sine) / root
    weights = jnp.where(mode_index == 0, 1.0, 2.0)
    analysis = jnp.where(even_rows, weights * cosine, 2.0 * sine) * (root / columns)
    analysis = jnp.where(mode_index < kept_modes, analysis, 0.0)
    return (synthesis, analysis)


def body(start_states, radial_inverse, offsets, mode_count):
    groups, components, axial_rows, radial_rows, columns = start_states.shape
    local_modes = radial_inverse.shape[0]
    ax_count = lax.axis_size("ax")
    classes = lax.axis_size("rad")
    radial_total = radial_rows * classes
    class_modes = columns // 2 // classes
    slots, keep, order = mode_classes(ax_count, local_modes, classes)

    parity = lax.axis_index("ax") % 2
    me = lax.axis_index("rad")
    own = jnp.asarray(slots)[parity, me]
    contribution = jnp.take(radial_inverse, own, axis=0)
    gathered = lax.all_gather(contribution, "ax", axis=0, tiled=False)
    gathered = gathered.reshape(ax_count // 2, 4, radial_total, radial_total)
    chosen = jnp.take(gathered, jnp.asarray(keep)[me], axis=1)
    operators = chosen.reshape(class_modes, classes, radial_rows, classes, radial_rows)

    natural = np.arange(columns, dtype=np.int32)
    synthesis_first, _ = fourier_tables(columns, mode_count[0], natural)
    synthesis, analysis = fourier_tables(columns, mode_count[0], order)
    radius = (
        (lax.axis_index("rad") * radial_rows + jnp.arange(radial_rows)).astype(jnp.float32) + 0.5
    ) / radial_total
    profile = (1.0 - radius * radius).reshape(1, 1, 1, radial_rows, 1)
    following = passed_along(start_states[0], "seg", -1)
    vectors = groups * components * axial_rows
    current = start_states
    for step_index in range(STEPS):
        if step_index == 0:
            physical = jnp.einsum("gczrj,jp->gczrp", current, synthesis_first, precision=highest)
        else:
            physical = jnp.einsum("jgczr,jp->gczrp", current, synthesis, precision=highest)
        padded = padded_2(physical, (("ax", 2),), 1)
        gradient = (padded[:, :, 2:] - padded[:, :, :-2]) * 20.0
        advecting = profile + padded[:, 2:3, 1:-1]
        forcing = physical - 0.02 * advecting * gradient
        spectral = jnp.einsum("gczrp,jp->jgczr", forcing, analysis, precision=highest)
        spectral = spectral.reshape(classes, class_modes, 2, vectors, radial_rows)
        pencils = lax.all_to_all(spectral, "rad", 0, 0, tiled=False)
        solved = jnp.einsum(
            "mQRqs,qmkvs->QmkvR", operators, pencils, precision=highest
        )
        returned = lax.all_to_all(solved, "rad", 0, 0, tiled=False)
        current = returned.reshape(columns, groups, components, axial_rows, radial_rows)

    chunk = columns // ax_count
    blocks = current.reshape(ax_count, chunk, groups, components, axial_rows, radial_rows)
    blocks = lax.all_to_all(blocks, "ax", 0, 0, tiled=False)
    blocks = jnp.transpose(blocks, (1, 2, 3, 0, 4, 5)).reshape(
        chunk, groups, components, ax_count * axial_rows, radial_rows
    )
    shifted = [jnp.roll(blocks[:, member], offsets[member], axis=2) for member in range(groups)]
    blocks = jnp.stack(shifted, axis=1).reshape(
        chunk, groups, components, ax_count, axial_rows, radial_rows
    )
    blocks = jnp.transpose(blocks, (3, 0, 1, 2, 4, 5))
    blocks = lax.all_to_all(blocks, "ax", 0, 0, tiled=False)
    ending = blocks.reshape(columns, groups, components, axial_rows, radial_rows)
    inverse = np.argsort(order).astype(np.int32)
    ending = jnp.take(ending, jnp.asarray(inverse), axis=0)
    ending = jnp.transpose(ending, (1, 2, 3, 4, 0))
    upcoming = jnp.concatenate([start_states[1:], following[None]], axis=0)
    return ending - upcoming


def solution(mesh):
    placed = (P("seg", None, "ax", "rad", None), P("ax", None, None), P("seg"), P())
    return jax.shard_map(
        body,
        mesh=mesh,
        in_specs=placed,
        out_specs=P("seg", None, "ax", "rad", None),
        check_vma=False,
    )
```

```python
import functools
import math

import numpy as np
import jax
import jax.numpy as jnp
from jax import lax
from jax.experimental import pallas as pl
from jax.experimental.pallas import tpu as pltpu
from jax.sharding import PartitionSpec as P

STEPS = 2


highest = lax.Precision.HIGHEST
MESH_ID = pl.DeviceIdType.MESH


def passed_along(value, axis, steps):
    count = lax.axis_size(axis)
    pairs = [(source, (source + steps) % count) for source in range(count)]
    return lax.ppermute(value, axis, pairs)


def padded_2(array, sides, width):
    for axis, dim in sides:
        peers, length = (lax.axis_size(axis), array.shape[dim])
        up = [(i, (i + 1) % peers) for i in range(peers)]
        down = [(j, i) for i, j in up]
        last = lax.slice_in_dim(array, length - width, length, axis=dim)
        leading = lax.slice_in_dim(array, 0, width, axis=dim)
        before = lax.ppermute(last, axis, up)
        after = lax.ppermute(leading, axis, down)
        array = jnp.concatenate([before, array, after], axis=dim)
    return array


def exchange_kernel(axis, count, x_ref, o_ref, send_sem, recv_sem, local_sem):
    me = lax.axis_index(axis)
    barrier = pltpu.get_barrier_semaphore()
    for step in range(1, count):
        pl.semaphore_signal(
            barrier, inc=1, device_id={axis: (me + step) % count}, device_id_type=MESH_ID
        )
    pl.semaphore_wait(barrier, count - 1)
    local = pltpu.make_async_copy(x_ref.at[me], o_ref.at[me], local_sem)
    local.start()
    copies = []
    for step in range(1, count):
        peer = (me + step) % count
        copy = pltpu.make_async_remote_copy(
            src_ref=x_ref.at[peer],
            dst_ref=o_ref.at[me],
            send_sem=send_sem.at[step - 1],
            recv_sem=recv_sem.at[step - 1],
            device_id={axis: peer},
            device_id_type=MESH_ID,
        )
        copy.start()
        copies.append(copy)
    local.wait()
    for copy in copies:
        copy.wait()


def exchange(x, axis, collective_id):
    count = x.shape[0]
    return pl.pallas_call(
        functools.partial(exchange_kernel, axis, count),
        out_shape=jax.ShapeDtypeStruct(x.shape, x.dtype),
        in_specs=[pl.BlockSpec(memory_space=pl.ANY)],
        out_specs=pl.BlockSpec(memory_space=pl.ANY),
        scratch_shapes=[
            pltpu.SemaphoreType.DMA((count - 1,)),
            pltpu.SemaphoreType.DMA((count - 1,)),
            pltpu.SemaphoreType.DMA,
        ],
        compiler_params=pltpu.CompilerParams(
            collective_id=collective_id, has_side_effects=True
        ),
    )(x)


def mode_classes(ax_count, local_modes, classes):
    assert local_modes == 6 and classes == 4 and ax_count % 2 == 0
    starts = np.array([[0, 2, 4, 4], [0, 0, 2, 4]], np.int32)
    class_modes = []
    for q in range(classes):
        modes = []
        for pair in range(ax_count // 2):
            flat = [
                (2 * pair + parity) * local_modes + starts[parity][q] + slot
                for parity in range(2)
                for slot in range(2)
            ]
            modes.extend(flat[u] for u in range(4) if u != 3 - q)
        class_modes.append(modes)
    class_modes = np.array(class_modes, np.int32)
    columns = np.stack([2 * class_modes, 2 * class_modes + 1], axis=-1).reshape(-1)
    within = (class_modes.reshape(classes, ax_count // 2, 3) % (2 * local_modes))
    assert (within == within[:, :1]).all()
    return starts, columns, within[:, 0]


def fourier_tables(columns, kept_modes, order):
    modes_total = columns // 2
    row_index = jnp.asarray(order)[:, None]
    point_index = lax.broadcasted_iota(jnp.int32, (columns, columns), 1)
    mode_index = row_index // 2
    phase = (mode_index * point_index % columns).astype(jnp.float32) * (2.0 * math.pi / columns)
    even_rows = row_index % 2 == 0
    cosine = jnp.cos(phase)
    sine = jnp.sin(phase)
    root = math.sqrt(modes_total)
    synthesis = jnp.where(even_rows, cosine, sine) / root
    weights = jnp.where(mode_index == 0, 1.0, 2.0)
    analysis = jnp.where(even_rows, weights * cosine, 2.0 * sine) * (root / columns)
    analysis = jnp.where(mode_index < kept_modes, analysis, 0.0)
    return (synthesis, analysis)


def body(start_states, radial_inverse, offsets, mode_count):
    groups, components, axial_rows, radial_rows, columns = start_states.shape
    local_modes = radial_inverse.shape[0]
    ax_count = lax.axis_size("ax")
    classes = lax.axis_size("rad")
    radial_total = radial_rows * classes
    class_modes = columns // 2 // classes
    vectors = groups * components * axial_rows
    lanes = vectors * radial_rows
    starts, order, within = mode_classes(ax_count, local_modes, classes)

    parity = lax.axis_index("ax") % 2
    me = lax.axis_index("rad")
    start = jnp.asarray(starts)[parity, me]
    contribution = lax.dynamic_slice_in_dim(radial_inverse, start, 2, axis=0)
    gathered = lax.all_gather(contribution, "ax", axis=0, tiled=False)
    gathered = gathered.reshape(ax_count // 2, 4, radial_total, radial_total)
    slot = lax.broadcasted_iota(jnp.int32, (1, 3, 1, 1), 1)
    operators = jnp.where(slot < 3 - me, gathered[:, 0:3], gathered[:, 1:4])
    operators = operators.reshape(class_modes, radial_total, radial_total)

    natural = np.arange(columns, dtype=np.int32)
    synthesis_first, _ = fourier_tables(columns, mode_count[0], natural)
    synthesis, analysis = fourier_tables(columns, mode_count[0], order)
    radius = (
        (lax.axis_index("rad") * radial_rows + jnp.arange(radial_rows)).astype(jnp.float32) + 0.5
    ) / radial_total
    profile = (1.0 - radius * radius).reshape(1, 1, 1, radial_rows, 1)
    following = passed_along(start_states[0], "seg", -1)
    current = start_states.reshape(lanes, columns)
    for step_index in range(STEPS):
        if step_index == 0:
            physical = jnp.dot(current, synthesis_first, precision=highest)
        else:
            physical = jnp.einsum("jn,jp->np", current, synthesis, precision=highest)
        physical = physical.reshape(groups, components, axial_rows, radial_rows, columns)
        padded = padded_2(physical, (("ax", 2),), 1)
        gradient = (padded[:, :, 2:] - padded[:, :, :-2]) * 20.0
        advecting = profile + padded[:, 2:3, 1:-1]
        forcing = physical - 0.02 * advecting * gradient
        forcing = forcing.reshape(lanes, columns)
        spectral = jnp.einsum("np,jp->jn", forcing, analysis, precision=highest)
        spectral = spectral.reshape(classes, 2 * class_modes, lanes)
        pencils = exchange(spectral, "rad", 0)
        pencils = pencils.reshape(classes, class_modes, 2 * vectors, radial_rows)
        pencils = jnp.transpose(pencils, (1, 2, 0, 3)).reshape(
            class_modes, 2 * vectors, radial_total
        )
        solved = jnp.einsum("mns,mrs->mnr", pencils, operators, precision=highest)
        solved = solved.reshape(class_modes, 2 * vectors, classes, radial_rows)
        solved = jnp.transpose(solved, (2, 0, 1, 3)).reshape(classes, 2 * class_modes, lanes)
        returned = exchange(solved, "rad", 0)
        current = returned.reshape(columns, lanes)

    chunk = columns // ax_count
    blocks = exchange(current.reshape(ax_count, chunk, lanes), "ax", 1)
    blocks = blocks.reshape(ax_count, chunk, groups, components, axial_rows, radial_rows)
    blocks = jnp.transpose(blocks, (1, 2, 3, 0, 4, 5)).reshape(
        chunk, groups, components, ax_count * axial_rows, radial_rows
    )
    shifted = [jnp.roll(blocks[:, member], offsets[member], axis=2) for member in range(groups)]
    blocks = jnp.stack(shifted, axis=1).reshape(
        chunk, groups, components, ax_count, axial_rows, radial_rows
    )
    blocks = jnp.transpose(blocks, (3, 0, 1, 2, 4, 5)).reshape(ax_count, chunk, lanes)
    ending = exchange(blocks, "ax", 1)

    pairs = ax_count // 2
    ending = ending.reshape(classes, pairs, 3, 2, lanes)
    place = {int(within[q][u]): (q, u) for q in range(classes) for u in range(3)}
    ending = jnp.stack([ending[place[w][0], :, place[w][1]] for w in range(4 * 3)], axis=1)
    ending = ending.reshape(columns, lanes)
    ending = jnp.transpose(ending).reshape(groups, components, axial_rows, radial_rows, columns)
    upcoming = jnp.concatenate([start_states[1:], following[None]], axis=0)
    return ending - upcoming


def solution(mesh):
    placed = (P("seg", None, "ax", "rad", None), P("ax", None, None), P("seg"), P())
    return jax.shard_map(
        body,
        mesh=mesh,
        in_specs=placed,
        out_specs=P("seg", None, "ax", "rad", None),
        check_vma=False,
    )
```

```python
import functools
import math

import numpy as np
import jax
import jax.numpy as jnp
from jax import lax
from jax.experimental import pallas as pl
from jax.experimental.pallas import tpu as pltpu
from jax.sharding import PartitionSpec as P

STEPS = 2


highest = lax.Precision.HIGH
MESH_ID = pl.DeviceIdType.MESH


def passed_along(value, axis, steps):
    count = lax.axis_size(axis)
    pairs = [(source, (source + steps) % count) for source in range(count)]
    return lax.ppermute(value, axis, pairs)


def padded_2(array, sides, width):
    for axis, dim in sides:
        peers, length = (lax.axis_size(axis), array.shape[dim])
        up = [(i, (i + 1) % peers) for i in range(peers)]
        down = [(j, i) for i, j in up]
        last = lax.slice_in_dim(array, length - width, length, axis=dim)
        leading = lax.slice_in_dim(array, 0, width, axis=dim)
        before = lax.ppermute(last, axis, up)
        after = lax.ppermute(leading, axis, down)
        array = jnp.concatenate([before, array, after], axis=dim)
    return array


def exchange_kernel(axis, count, x_ref, o_ref, send_sem, recv_sem, local_sem):
    me = lax.axis_index(axis)
    barrier = pltpu.get_barrier_semaphore()
    for step in range(1, count):
        pl.semaphore_signal(
            barrier, inc=1, device_id={axis: (me + step) % count}, device_id_type=MESH_ID
        )
    pl.semaphore_wait(barrier, count - 1)
    local = pltpu.make_async_copy(x_ref.at[me], o_ref.at[me], local_sem)
    local.start()
    copies = []
    for step in range(1, count):
        peer = (me + step) % count
        copy = pltpu.make_async_remote_copy(
            src_ref=x_ref.at[peer],
            dst_ref=o_ref.at[me],
            send_sem=send_sem.at[step - 1],
            recv_sem=recv_sem.at[step - 1],
            device_id={axis: peer},
            device_id_type=MESH_ID,
        )
        copy.start()
        copies.append(copy)
    local.wait()
    for copy in copies:
        copy.wait()


def exchange(x, axis, collective_id):
    count = x.shape[0]
    return pl.pallas_call(
        functools.partial(exchange_kernel, axis, count),
        out_shape=jax.ShapeDtypeStruct(x.shape, x.dtype),
        in_specs=[pl.BlockSpec(memory_space=pl.ANY)],
        out_specs=pl.BlockSpec(memory_space=pl.ANY),
        scratch_shapes=[
            pltpu.SemaphoreType.DMA((count - 1,)),
            pltpu.SemaphoreType.DMA((count - 1,)),
            pltpu.SemaphoreType.DMA,
        ],
        compiler_params=pltpu.CompilerParams(
            collective_id=collective_id, has_side_effects=True
        ),
    )(x)


def mode_classes(ax_count, local_modes, classes):
    assert local_modes == 6 and classes == 4 and ax_count % 2 == 0
    starts = np.array([[0, 2, 4, 4], [0, 0, 2, 4]], np.int32)
    class_modes = []
    for q in range(classes):
        modes = []
        for pair in range(ax_count // 2):
            flat = [
                (2 * pair + parity) * local_modes + starts[parity][q] + slot
                for parity in range(2)
                for slot in range(2)
            ]
            modes.extend(flat[u] for u in range(4) if u != 3 - q)
        class_modes.append(modes)
    class_modes = np.array(class_modes, np.int32)
    columns = np.stack([2 * class_modes, 2 * class_modes + 1], axis=-1).reshape(-1)
    within = (class_modes.reshape(classes, ax_count // 2, 3) % (2 * local_modes))
    assert (within == within[:, :1]).all()
    return starts, columns, within[:, 0]


def fourier_tables(columns, kept_modes, order):
    modes_total = columns // 2
    row_index = jnp.asarray(order)[:, None]
    point_index = lax.broadcasted_iota(jnp.int32, (columns, columns), 1)
    mode_index = row_index // 2
    phase = (mode_index * point_index % columns).astype(jnp.float32) * (2.0 * math.pi / columns)
    even_rows = row_index % 2 == 0
    cosine = jnp.cos(phase)
    sine = jnp.sin(phase)
    root = math.sqrt(modes_total)
    synthesis = jnp.where(even_rows, cosine, sine) / root
    weights = jnp.where(mode_index == 0, 1.0, 2.0)
    analysis = jnp.where(even_rows, weights * cosine, 2.0 * sine) * (root / columns)
    analysis = jnp.where(mode_index < kept_modes, analysis, 0.0)
    return (synthesis, analysis)


def body(start_states, radial_inverse, offsets, mode_count):
    groups, components, axial_rows, radial_rows, columns = start_states.shape
    local_modes = radial_inverse.shape[0]
    ax_count = lax.axis_size("ax")
    classes = lax.axis_size("rad")
    radial_total = radial_rows * classes
    class_modes = columns // 2 // classes
    vectors = groups * components * axial_rows
    lanes = vectors * radial_rows
    starts, order, within = mode_classes(ax_count, local_modes, classes)

    parity = lax.axis_index("ax") % 2
    me = lax.axis_index("rad")
    start = jnp.asarray(starts)[parity, me]
    contribution = lax.dynamic_slice_in_dim(radial_inverse, start, 2, axis=0)
    gathered = lax.all_gather(contribution, "ax", axis=0, tiled=False)
    gathered = gathered.reshape(ax_count // 2, 4, radial_total, radial_total)
    slot = lax.broadcasted_iota(jnp.int32, (1, 3, 1, 1), 1)
    operators = jnp.where(slot < 3 - me, gathered[:, 0:3], gathered[:, 1:4])
    operators = operators.reshape(class_modes, radial_total, radial_total)

    natural = np.arange(columns, dtype=np.int32)
    synthesis_first, _ = fourier_tables(columns, mode_count[0], natural)
    synthesis, analysis = fourier_tables(columns, mode_count[0], order)
    radius = (
        (lax.axis_index("rad") * radial_rows + jnp.arange(radial_rows)).astype(jnp.float32) + 0.5
    ) / radial_total
    profile = (1.0 - radius * radius).reshape(1, 1, 1, radial_rows, 1)
    following = passed_along(start_states[0], "seg", -1)
    current = start_states.reshape(lanes, columns)
    for step_index in range(STEPS):
        if step_index == 0:
            physical = jnp.dot(current, synthesis_first, precision=highest)
        else:
            physical = jnp.einsum("jn,jp->np", current, synthesis, precision=highest)
        physical = physical.reshape(groups, components, axial_rows, radial_rows, columns)
        padded = padded_2(physical, (("ax", 2),), 1)
        gradient = (padded[:, :, 2:] - padded[:, :, :-2]) * 20.0
        advecting = profile + padded[:, 2:3, 1:-1]
        forcing = physical - 0.02 * advecting * gradient
        forcing = forcing.reshape(lanes, columns)
        spectral = jnp.einsum("np,jp->jn", forcing, analysis, precision=highest)
        spectral = spectral.reshape(classes, 2 * class_modes, lanes)
        pencils = exchange(spectral, "rad", 0)
        pencils = pencils.reshape(classes, class_modes, 2 * vectors, radial_rows)
        pencils = jnp.transpose(pencils, (1, 2, 0, 3)).reshape(
            class_modes, 2 * vectors, radial_total
        )
        solved = jnp.einsum("mns,mrs->mnr", pencils, operators, precision=highest)
        solved = solved.reshape(class_modes, 2 * vectors, classes, radial_rows)
        solved = jnp.transpose(solved, (2, 0, 1, 3)).reshape(classes, 2 * class_modes, lanes)
        returned = exchange(solved, "rad", 0)
        current = returned.reshape(columns, lanes)

    chunk = columns // ax_count
    blocks = exchange(current.reshape(ax_count, chunk, lanes), "ax", 1)
    blocks = blocks.reshape(ax_count, chunk, groups, components, axial_rows, radial_rows)
    blocks = jnp.transpose(blocks, (1, 2, 3, 0, 4, 5)).reshape(
        chunk, groups, components, ax_count * axial_rows, radial_rows
    )
    shifted = [jnp.roll(blocks[:, member], offsets[member], axis=2) for member in range(groups)]
    blocks = jnp.stack(shifted, axis=1).reshape(
        chunk, groups, components, ax_count, axial_rows, radial_rows
    )
    blocks = jnp.transpose(blocks, (3, 0, 1, 2, 4, 5)).reshape(ax_count, chunk, lanes)
    ending = exchange(blocks, "ax", 1)

    pairs = ax_count // 2
    ending = ending.reshape(classes, pairs, 3, 2, lanes)
    place = {int(within[q][u]): (q, u) for q in range(classes) for u in range(3)}
    ending = jnp.stack([ending[place[w][0], :, place[w][1]] for w in range(4 * 3)], axis=1)
    ending = ending.reshape(columns, lanes)
    ending = jnp.transpose(ending).reshape(groups, components, axial_rows, radial_rows, columns)
    upcoming = jnp.concatenate([start_states[1:], following[None]], axis=0)
    return ending - upcoming


def solution(mesh):
    placed = (P("seg", None, "ax", "rad", None), P("ax", None, None), P("seg"), P())
    return jax.shard_map(
        body,
        mesh=mesh,
        in_specs=placed,
        out_specs=P("seg", None, "ax", "rad", None),
        check_vma=False,
    )
```

```python
import functools
import math

import numpy as np
import jax
import jax.numpy as jnp
from jax import lax
from jax.experimental import pallas as pl
from jax.experimental.pallas import tpu as pltpu
from jax.sharding import PartitionSpec as P

STEPS = 2


highest = lax.Precision.HIGHEST
MESH_ID = pl.DeviceIdType.MESH


def passed_along(value, axis, steps):
    count = lax.axis_size(axis)
    pairs = [(source, (source + steps) % count) for source in range(count)]
    return lax.ppermute(value, axis, pairs)


def padded_2(array, sides, width):
    for axis, dim in sides:
        peers, length = (lax.axis_size(axis), array.shape[dim])
        up = [(i, (i + 1) % peers) for i in range(peers)]
        down = [(j, i) for i, j in up]
        last = lax.slice_in_dim(array, length - width, length, axis=dim)
        leading = lax.slice_in_dim(array, 0, width, axis=dim)
        before = lax.ppermute(last, axis, up)
        after = lax.ppermute(leading, axis, down)
        array = jnp.concatenate([before, array, after], axis=dim)
    return array


def exchange_kernel(axis, count, x_ref, o_ref, send_sem, recv_sem, local_sem):
    me = lax.axis_index(axis)
    barrier = pltpu.get_barrier_semaphore()
    for step in range(1, count):
        pl.semaphore_signal(
            barrier, inc=1, device_id={axis: (me + step) % count}, device_id_type=MESH_ID
        )
    pl.semaphore_wait(barrier, count - 1)
    local = pltpu.make_async_copy(x_ref.at[me], o_ref.at[me], local_sem)
    local.start()
    copies = []
    for step in range(1, count):
        hop = (step + 1) // 2 if step % 2 else count - step // 2
        peer = (me + hop) % count
        copy = pltpu.make_async_remote_copy(
            src_ref=x_ref.at[peer],
            dst_ref=o_ref.at[me],
            send_sem=send_sem.at[step - 1],
            recv_sem=recv_sem.at[step - 1],
            device_id={axis: peer},
            device_id_type=MESH_ID,
        )
        copy.start()
        copies.append(copy)
    local.wait()
    for copy in copies:
        copy.wait()


def exchange(x, axis, collective_id):
    count = x.shape[0]
    return pl.pallas_call(
        functools.partial(exchange_kernel, axis, count),
        out_shape=jax.ShapeDtypeStruct(x.shape, x.dtype),
        in_specs=[pl.BlockSpec(memory_space=pl.ANY)],
        out_specs=pl.BlockSpec(memory_space=pl.ANY),
        scratch_shapes=[
            pltpu.SemaphoreType.DMA((count - 1,)),
            pltpu.SemaphoreType.DMA((count - 1,)),
            pltpu.SemaphoreType.DMA,
        ],
        compiler_params=pltpu.CompilerParams(
            collective_id=collective_id, has_side_effects=True
        ),
    )(x)


def mode_classes(ax_count, local_modes, classes):
    assert local_modes == 6 and classes == 4 and ax_count % 2 == 0
    starts = np.array([[0, 2, 3, 4], [0, 1, 2, 4]], np.int32)
    class_modes = []
    for q in range(classes):
        modes = []
        for pair in range(ax_count // 2):
            flat = [
                (2 * pair + parity) * local_modes + starts[parity][q] + slot
                for parity in range(2)
                for slot in range(2)
            ]
            modes.extend(flat[u] for u in range(4) if u != (0 if q >= 2 else 3))
        class_modes.append(modes)
    class_modes = np.array(class_modes, np.int32)
    columns = np.stack([2 * class_modes, 2 * class_modes + 1], axis=-1).reshape(-1)
    within = (class_modes.reshape(classes, ax_count // 2, 3) % (2 * local_modes))
    assert (within == within[:, :1]).all()
    return starts, columns, within[:, 0]


def fourier_tables(columns, kept_modes, order):
    modes_total = columns // 2
    row_index = jnp.asarray(order)[:, None]
    point_index = lax.broadcasted_iota(jnp.int32, (columns, columns), 1)
    mode_index = row_index // 2
    phase = (mode_index * point_index % columns).astype(jnp.float32) * (2.0 * math.pi / columns)
    even_rows = row_index % 2 == 0
    cosine = jnp.cos(phase)
    sine = jnp.sin(phase)
    root = math.sqrt(modes_total)
    synthesis = jnp.where(even_rows, cosine, sine) / root
    weights = jnp.where(mode_index == 0, 1.0, 2.0)
    analysis = jnp.where(even_rows, weights * cosine, 2.0 * sine) * (root / columns)
    analysis = jnp.where(mode_index < kept_modes, analysis, 0.0)
    return (synthesis, analysis)


def body(start_states, radial_inverse, offsets, mode_count):
    groups, components, axial_rows, radial_rows, columns = start_states.shape
    local_modes = radial_inverse.shape[0]
    ax_count = lax.axis_size("ax")
    classes = lax.axis_size("rad")
    radial_total = radial_rows * classes
    class_modes = columns // 2 // classes
    vectors = groups * components * axial_rows
    lanes = vectors * radial_rows
    starts, order, within = mode_classes(ax_count, local_modes, classes)

    parity = lax.axis_index("ax") % 2
    me = lax.axis_index("rad")
    start = jnp.asarray(starts)[parity, me]
    contribution = lax.dynamic_slice_in_dim(radial_inverse, start, 2, axis=0)
    gathered = lax.all_gather(contribution, "ax", axis=0, tiled=False)
    gathered = gathered.reshape(ax_count // 2, 4, radial_total, radial_total)
    window = (me >= 2).astype(jnp.int32)
    operators = lax.dynamic_slice_in_dim(gathered, window, 3, axis=1)
    operators = operators.reshape(class_modes, radial_total, radial_total)

    natural = np.arange(columns, dtype=np.int32)
    synthesis_first, _ = fourier_tables(columns, mode_count[0], natural)
    synthesis, analysis = fourier_tables(columns, mode_count[0], order)
    radius = (
        (lax.axis_index("rad") * radial_rows + jnp.arange(radial_rows)).astype(jnp.float32) + 0.5
    ) / radial_total
    profile = (1.0 - radius * radius).reshape(1, 1, 1, radial_rows, 1)
    following = passed_along(start_states[0], "seg", -1)
    current = start_states.reshape(lanes, columns)
    for step_index in range(STEPS):
        if step_index == 0:
            physical = jnp.dot(current, synthesis_first, precision=highest)
        else:
            physical = jnp.einsum("jn,jp->np", current, synthesis, precision=highest)
        physical = physical.reshape(groups, components, axial_rows, radial_rows, columns)
        padded = padded_2(physical, (("ax", 2),), 1)
        gradient = (padded[:, :, 2:] - padded[:, :, :-2]) * 20.0
        advecting = profile + padded[:, 2:3, 1:-1]
        forcing = physical - 0.02 * advecting * gradient
        forcing = forcing.reshape(lanes, columns)
        spectral = jnp.einsum("np,jp->jn", forcing, analysis, precision=highest)
        spectral = spectral.reshape(classes, 2 * class_modes, lanes)
        pencils = exchange(spectral, "rad", 0)
        pencils = pencils.reshape(classes, class_modes, 2 * vectors, radial_rows)
        pencils = jnp.transpose(pencils, (1, 2, 0, 3)).reshape(
            class_modes, 2 * vectors, radial_total
        )
        solved = jnp.einsum("mns,mrs->mnr", pencils, operators, precision=highest)
        solved = solved.reshape(class_modes, 2 * vectors, classes, radial_rows)
        solved = jnp.transpose(solved, (2, 0, 1, 3)).reshape(classes, 2 * class_modes, lanes)
        returned = exchange(solved, "rad", 0)
        current = returned.reshape(columns, lanes)

    chunk = columns // ax_count
    blocks = exchange(current.reshape(ax_count, chunk, lanes), "ax", 1)
    blocks = blocks.reshape(ax_count, chunk, groups, components, axial_rows, radial_rows)
    blocks = jnp.transpose(blocks, (1, 2, 3, 0, 4, 5)).reshape(
        chunk, groups, components, ax_count * axial_rows, radial_rows
    )
    shifted = [jnp.roll(blocks[:, member], offsets[member], axis=2) for member in range(groups)]
    blocks = jnp.stack(shifted, axis=1).reshape(
        chunk, groups, components, ax_count, axial_rows, radial_rows
    )
    blocks = jnp.transpose(blocks, (3, 0, 1, 2, 4, 5)).reshape(ax_count, chunk, lanes)
    ending = exchange(blocks, "ax", 1)

    pairs = ax_count // 2
    ending = ending.reshape(classes, pairs, 3, 2, lanes)
    place = {int(within[q][u]): (q, u) for q in range(classes) for u in range(3)}
    ending = jnp.stack([ending[place[w][0], :, place[w][1]] for w in range(4 * 3)], axis=1)
    ending = ending.reshape(columns, lanes)
    ending = jnp.transpose(ending).reshape(groups, components, axial_rows, radial_rows, columns)
    upcoming = jnp.concatenate([start_states[1:], following[None]], axis=0)
    return ending - upcoming


def solution(mesh):
    placed = (P("seg", None, "ax", "rad", None), P("ax", None, None), P("seg"), P())
    return jax.shard_map(
        body,
        mesh=mesh,
        in_specs=placed,
        out_specs=P("seg", None, "ax", "rad", None),
        check_vma=False,
    )
```

```python
import functools
import math

import numpy as np
import jax
import jax.numpy as jnp
from jax import lax
from jax.experimental import pallas as pl
from jax.experimental.pallas import tpu as pltpu
from jax.sharding import PartitionSpec as P

STEPS = 2


highest = lax.Precision.HIGHEST
MESH_ID = pl.DeviceIdType.MESH


def passed_along(value, axis, steps):
    count = lax.axis_size(axis)
    pairs = [(source, (source + steps) % count) for source in range(count)]
    return lax.ppermute(value, axis, pairs)


def padded_2(array, sides, width):
    for axis, dim in sides:
        peers, length = (lax.axis_size(axis), array.shape[dim])
        up = [(i, (i + 1) % peers) for i in range(peers)]
        down = [(j, i) for i, j in up]
        last = lax.slice_in_dim(array, length - width, length, axis=dim)
        leading = lax.slice_in_dim(array, 0, width, axis=dim)
        before = lax.ppermute(last, axis, up)
        after = lax.ppermute(leading, axis, down)
        array = jnp.concatenate([before, array, after], axis=dim)
    return array


def exchange_kernel(axis, count, x_ref, o_ref, send_sem, recv_sem, local_sem):
    me = lax.axis_index(axis)
    barrier = pltpu.get_barrier_semaphore()
    for step in range(1, count):
        pl.semaphore_signal(
            barrier, inc=1, device_id={axis: (me + step) % count}, device_id_type=MESH_ID
        )
    pl.semaphore_wait(barrier, count - 1)
    local = pltpu.make_async_copy(x_ref.at[me], o_ref.at[me], local_sem)
    local.start()
    copies = []
    for step in range(1, count):
        hop = (step + 1) // 2 if step % 2 else count - step // 2
        peer = (me + hop) % count
        copy = pltpu.make_async_remote_copy(
            src_ref=x_ref.at[peer],
            dst_ref=o_ref.at[me],
            send_sem=send_sem.at[step - 1],
            recv_sem=recv_sem.at[step - 1],
            device_id={axis: peer},
            device_id_type=MESH_ID,
        )
        copy.start()
        copies.append(copy)
    local.wait()
    for copy in copies:
        copy.wait()


def exchange(x, axis, collective_id):
    count = x.shape[0]
    return pl.pallas_call(
        functools.partial(exchange_kernel, axis, count),
        out_shape=jax.ShapeDtypeStruct(x.shape, x.dtype),
        in_specs=[pl.BlockSpec(memory_space=pl.ANY)],
        out_specs=pl.BlockSpec(memory_space=pl.ANY),
        scratch_shapes=[
            pltpu.SemaphoreType.DMA((count - 1,)),
            pltpu.SemaphoreType.DMA((count - 1,)),
            pltpu.SemaphoreType.DMA,
        ],
        compiler_params=pltpu.CompilerParams(
            collective_id=collective_id, has_side_effects=True
        ),
    )(x)


def rolled_axially(current, offsets, shape):
    groups, components, axial_rows, radial_rows = shape
    columns, lanes = current.shape
    ax_count = lax.axis_size("ax")
    chunk = columns // ax_count
    blocks = exchange(current.reshape(ax_count, chunk, lanes), "ax", 1)
    blocks = blocks.reshape(ax_count, chunk, groups, components, axial_rows, radial_rows)
    blocks = jnp.transpose(blocks, (1, 2, 3, 0, 4, 5)).reshape(
        chunk, groups, components, ax_count * axial_rows, radial_rows
    )
    shifted = [jnp.roll(blocks[:, member], offsets[member], axis=2) for member in range(groups)]
    blocks = jnp.stack(shifted, axis=1).reshape(
        chunk, groups, components, ax_count, axial_rows, radial_rows
    )
    blocks = jnp.transpose(blocks, (3, 0, 1, 2, 4, 5)).reshape(ax_count, chunk, lanes)
    return exchange(blocks, "ax", 1).reshape(columns, lanes)


def mode_classes(ax_count, local_modes, classes):
    assert local_modes == 6 and classes == 4 and ax_count % 2 == 0
    starts = np.array([[0, 2, 3, 4], [0, 1, 2, 4]], np.int32)
    class_modes = []
    for q in range(classes):
        modes = []
        for pair in range(ax_count // 2):
            flat = [
                (2 * pair + parity) * local_modes + starts[parity][q] + slot
                for parity in range(2)
                for slot in range(2)
            ]
            modes.extend(flat[u] for u in range(4) if u != (0 if q >= 2 else 3))
        class_modes.append(modes)
    class_modes = np.array(class_modes, np.int32)
    columns = np.stack([2 * class_modes, 2 * class_modes + 1], axis=-1).reshape(-1)
    within = (class_modes.reshape(classes, ax_count // 2, 3) % (2 * local_modes))
    assert (within == within[:, :1]).all()
    return starts, columns, within[:, 0]


def fourier_tables(columns, kept_modes, order):
    modes_total = columns // 2
    row_index = jnp.asarray(order)[:, None]
    point_index = lax.broadcasted_iota(jnp.int32, (columns, columns), 1)
    mode_index = row_index // 2
    phase = (mode_index * point_index % columns).astype(jnp.float32) * (2.0 * math.pi / columns)
    even_rows = row_index % 2 == 0
    cosine = jnp.cos(phase)
    sine = jnp.sin(phase)
    root = math.sqrt(modes_total)
    synthesis = jnp.where(even_rows, cosine, sine) / root
    weights = jnp.where(mode_index == 0, 1.0, 2.0)
    analysis = jnp.where(even_rows, weights * cosine, 2.0 * sine) * (root / columns)
    analysis = jnp.where(mode_index < kept_modes, analysis, 0.0)
    return (synthesis, analysis)


def body(start_states, radial_inverse, offsets, mode_count):
    groups, components, axial_rows, radial_rows, columns = start_states.shape
    local_modes = radial_inverse.shape[0]
    ax_count = lax.axis_size("ax")
    classes = lax.axis_size("rad")
    radial_total = radial_rows * classes
    class_modes = columns // 2 // classes
    vectors = groups * components * axial_rows
    lanes = vectors * radial_rows
    starts, order, within = mode_classes(ax_count, local_modes, classes)

    parity = lax.axis_index("ax") % 2
    me = lax.axis_index("rad")
    start = jnp.asarray(starts)[parity, me]
    contribution = lax.dynamic_slice_in_dim(radial_inverse, start, 2, axis=0)
    gathered = lax.all_gather(contribution, "ax", axis=0, tiled=False)
    gathered = gathered.reshape(ax_count // 2, 4, radial_total, radial_total)
    window = (me >= 2).astype(jnp.int32)
    operators = lax.dynamic_slice_in_dim(gathered, window, 3, axis=1)
    operators = operators.reshape(class_modes, radial_total, radial_total)

    natural = np.arange(columns, dtype=np.int32)
    synthesis_first, _ = fourier_tables(columns, mode_count[0], natural)
    synthesis, analysis = fourier_tables(columns, mode_count[0], order)
    radius = (
        (lax.axis_index("rad") * radial_rows + jnp.arange(radial_rows)).astype(jnp.float32) + 0.5
    ) / radial_total
    profile = (1.0 - radius * radius).reshape(1, 1, 1, radial_rows, 1)
    following = passed_along(start_states[0], "seg", -1)
    current = start_states.reshape(lanes, columns)
    for step_index in range(STEPS):
        if step_index == 0:
            physical = jnp.dot(current, synthesis_first, precision=highest)
        else:
            physical = jnp.einsum("jn,jp->np", current, synthesis, precision=highest)
        physical = physical.reshape(groups, components, axial_rows, radial_rows, columns)
        padded = padded_2(physical, (("ax", 2),), 1)
        gradient = (padded[:, :, 2:] - padded[:, :, :-2]) * 20.0
        advecting = profile + padded[:, 2:3, 1:-1]
        forcing = physical - 0.02 * advecting * gradient
        forcing = forcing.reshape(lanes, columns)
        spectral = jnp.einsum("np,jp->jn", forcing, analysis, precision=highest)
        spectral = spectral.reshape(classes, 2 * class_modes, lanes)
        pencils = exchange(spectral, "rad", 0)
        if step_index == 0:
            pencils = rolled_axially(
                pencils.reshape(columns, lanes),
                offsets,
                (groups, components, axial_rows, radial_rows),
            ).reshape(classes, 2 * class_modes, lanes)
        pencils = pencils.reshape(classes, class_modes, 2 * vectors, radial_rows)
        pencils = jnp.transpose(pencils, (1, 2, 0, 3)).reshape(
            class_modes, 2 * vectors, radial_total
        )
        solved = jnp.einsum("mns,mrs->mnr", pencils, operators, precision=highest)
        solved = solved.reshape(class_modes, 2 * vectors, classes, radial_rows)
        solved = jnp.transpose(solved, (2, 0, 1, 3)).reshape(classes, 2 * class_modes, lanes)
        returned = exchange(solved, "rad", 0)
        current = returned.reshape(columns, lanes)

    ending = current

    pairs = ax_count // 2
    ending = ending.reshape(classes, pairs, 3, 2, lanes)
    place = {int(within[q][u]): (q, u) for q in range(classes) for u in range(3)}
    ending = jnp.stack([ending[place[w][0], :, place[w][1]] for w in range(4 * 3)], axis=1)
    ending = ending.reshape(columns, lanes)
    ending = jnp.transpose(ending).reshape(groups, components, axial_rows, radial_rows, columns)
    upcoming = jnp.concatenate([start_states[1:], following[None]], axis=0)
    return ending - upcoming


def solution(mesh):
    placed = (P("seg", None, "ax", "rad", None), P("ax", None, None), P("seg"), P())
    return jax.shard_map(
        body,
        mesh=mesh,
        in_specs=placed,
        out_specs=P("seg", None, "ax", "rad", None),
        check_vma=False,
    )
```

```python
import functools
import math

import numpy as np
import jax
import jax.numpy as jnp
from jax import lax
from jax.experimental import pallas as pl
from jax.experimental.pallas import tpu as pltpu
from jax.sharding import PartitionSpec as P

STEPS = 2


highest = lax.Precision.HIGHEST
MESH_ID = pl.DeviceIdType.MESH


def passed_along(value, axis, steps):
    count = lax.axis_size(axis)
    pairs = [(source, (source + steps) % count) for source in range(count)]
    return lax.ppermute(value, axis, pairs)


def padded_2(array, sides, width):
    for axis, dim in sides:
        peers, length = (lax.axis_size(axis), array.shape[dim])
        up = [(i, (i + 1) % peers) for i in range(peers)]
        down = [(j, i) for i, j in up]
        last = lax.slice_in_dim(array, length - width, length, axis=dim)
        leading = lax.slice_in_dim(array, 0, width, axis=dim)
        before = lax.ppermute(last, axis, up)
        after = lax.ppermute(leading, axis, down)
        array = jnp.concatenate([before, array, after], axis=dim)
    return array


def exchange_kernel(axes, sizes, x_ref, o_ref, send_sem, recv_sem, local_sem):
    count = x_ref.shape[0]

    def place(index):
        coords = {}
        for axis, size in reversed(list(zip(axes, sizes))):
            coords[axis] = index % size
            index = index // size
        return coords

    me = 0
    for axis, size in zip(axes, sizes):
        me = me * size + lax.axis_index(axis)
    barrier = pltpu.get_barrier_semaphore()
    for step in range(1, count):
        pl.semaphore_signal(
            barrier, inc=1, device_id=place((me + step) % count), device_id_type=MESH_ID
        )
    pl.semaphore_wait(barrier, count - 1)
    local = pltpu.make_async_copy(x_ref.at[me], o_ref.at[me], local_sem)
    local.start()
    copies = []
    for step in range(1, count):
        hop = (step + 1) // 2 if step % 2 else count - step // 2
        peer = (me + hop) % count
        copy = pltpu.make_async_remote_copy(
            src_ref=x_ref.at[peer],
            dst_ref=o_ref.at[me],
            send_sem=send_sem.at[step - 1],
            recv_sem=recv_sem.at[step - 1],
            device_id=place(peer),
            device_id_type=MESH_ID,
        )
        copy.start()
        copies.append(copy)
    local.wait()
    for copy in copies:
        copy.wait()


def exchange(x, axes, collective_id):
    count = x.shape[0]
    sizes = tuple(lax.axis_size(axis) for axis in axes)
    return pl.pallas_call(
        functools.partial(exchange_kernel, axes, sizes),
        out_shape=jax.ShapeDtypeStruct(x.shape, x.dtype),
        in_specs=[pl.BlockSpec(memory_space=pl.ANY)],
        out_specs=pl.BlockSpec(memory_space=pl.ANY),
        scratch_shapes=[
            pltpu.SemaphoreType.DMA((count - 1,)),
            pltpu.SemaphoreType.DMA((count - 1,)),
            pltpu.SemaphoreType.DMA,
        ],
        compiler_params=pltpu.CompilerParams(
            collective_id=collective_id, has_side_effects=True
        ),
    )(x)


def mode_classes(ax_count, local_modes, classes):
    assert local_modes == 6 and classes == 8 and ax_count % 4 == 0
    slots = np.zeros((4, classes), np.int32)
    for d in range(4):
        given = [c for c in range(classes) if c // 2 != d]
        for index, c in enumerate(given):
            slots[d][c] = index
    class_modes = []
    for c in range(classes):
        modes = []
        for quad in range(ax_count // 4):
            for d in range(4):
                if d != c // 2:
                    modes.append((4 * quad + d) * local_modes + slots[d][c])
        class_modes.append(modes)
    class_modes = np.array(class_modes, np.int32)
    assert sorted(class_modes.reshape(-1).tolist()) == list(range(ax_count * local_modes))
    columns = np.stack([2 * class_modes, 2 * class_modes + 1], axis=-1).reshape(-1)
    return slots, columns


def fourier_tables(columns, kept_modes, order):
    modes_total = columns // 2
    row_index = jnp.asarray(order)[:, None]
    point_index = lax.broadcasted_iota(jnp.int32, (columns, columns), 1)
    mode_index = row_index // 2
    phase = (mode_index * point_index % columns).astype(jnp.float32) * (2.0 * math.pi / columns)
    even_rows = row_index % 2 == 0
    cosine = jnp.cos(phase)
    sine = jnp.sin(phase)
    root = math.sqrt(modes_total)
    synthesis = jnp.where(even_rows, cosine, sine) / root
    weights = jnp.where(mode_index == 0, 1.0, 2.0)
    analysis = jnp.where(even_rows, weights * cosine, 2.0 * sine) * (root / columns)
    analysis = jnp.where(mode_index < kept_modes, analysis, 0.0)
    return (synthesis, analysis)


def body(start_states, radial_inverse, offsets, mode_count):
    groups, components, axial_rows, radial_rows, columns = start_states.shape
    local_modes = radial_inverse.shape[0]
    ax_count = lax.axis_size("ax")
    seg_count = lax.axis_size("seg")
    rad_count = lax.axis_size("rad")
    classes = seg_count * rad_count
    radial_total = radial_rows * rad_count
    class_modes = columns // 2 // classes
    vectors = groups * components * axial_rows
    lanes = vectors * radial_rows
    slots, order = mode_classes(ax_count, local_modes, classes)
    ring = ("seg", "rad")

    me = lax.axis_index("seg") * rad_count + lax.axis_index("rad")
    own = jnp.asarray(slots)[lax.axis_index("ax") % 4, me]
    contribution = lax.dynamic_slice_in_dim(radial_inverse, own, 1, axis=0)
    gathered = lax.all_gather(contribution, "ax", axis=0, tiled=True)
    gathered = gathered.reshape(ax_count // 4, 4, radial_total, radial_total)
    slot = lax.broadcasted_iota(jnp.int32, (1, 3, 1, 1), 1)
    operators = jnp.where(slot < me // 2, gathered[:, 0:3], gathered[:, 1:4])
    operators = operators.reshape(class_modes, radial_total, radial_total)

    natural = np.arange(columns, dtype=np.int32)
    synthesis_first, _ = fourier_tables(columns, mode_count[0], natural)
    synthesis, analysis = fourier_tables(columns, mode_count[0], order)
    radius = (
        (lax.axis_index("rad") * radial_rows + jnp.arange(radial_rows)).astype(jnp.float32) + 0.5
    ) / radial_total
    profile = (1.0 - radius * radius).reshape(1, 1, 1, radial_rows, 1)
    following = passed_along(start_states[0], "seg", -1)
    current = start_states.reshape(lanes, columns)
    for step_index in range(STEPS):
        if step_index == 0:
            physical = jnp.dot(current, synthesis_first, precision=highest)
        else:
            physical = jnp.einsum("jn,jp->np", current, synthesis, precision=highest)
        physical = physical.reshape(groups, components, axial_rows, radial_rows, columns)
        padded = padded_2(physical, (("ax", 2),), 1)
        gradient = (padded[:, :, 2:] - padded[:, :, :-2]) * 20.0
        advecting = profile + padded[:, 2:3, 1:-1]
        forcing = physical - 0.02 * advecting * gradient
        forcing = forcing.reshape(lanes, columns)
        spectral = jnp.einsum("np,jp->jn", forcing, analysis, precision=highest)
        spectral = spectral.reshape(classes, 2 * class_modes, lanes)
        pencils = exchange(spectral, ring, 0)
        pencils = pencils.reshape(
            seg_count, rad_count, class_modes, 2 * vectors, radial_rows
        )
        pencils = jnp.transpose(pencils, (2, 0, 3, 1, 4)).reshape(
            class_modes, seg_count * 2 * vectors, radial_total
        )
        solved = jnp.einsum("mns,mrs->mnr", pencils, operators, precision=highest)
        solved = solved.reshape(class_modes, seg_count, 2 * vectors, rad_count, radial_rows)
        solved = jnp.transpose(solved, (1, 3, 0, 2, 4)).reshape(classes, 2 * class_modes, lanes)
        returned = exchange(solved, ring, 0)
        current = returned.reshape(columns, lanes)

    chunk = columns // ax_count
    blocks = exchange(current.reshape(ax_count, chunk, lanes), ("ax",), 1)
    blocks = blocks.reshape(ax_count, chunk, groups, components, axial_rows, radial_rows)
    blocks = jnp.transpose(blocks, (1, 2, 3, 0, 4, 5)).reshape(
        chunk, groups, components, ax_count * axial_rows, radial_rows
    )
    shifted = [jnp.roll(blocks[:, member], offsets[member], axis=2) for member in range(groups)]
    blocks = jnp.stack(shifted, axis=1).reshape(
        chunk, groups, components, ax_count, axial_rows, radial_rows
    )
    blocks = jnp.transpose(blocks, (3, 0, 1, 2, 4, 5)).reshape(ax_count, chunk, lanes)
    ending = exchange(blocks, ("ax",), 1).reshape(columns, lanes)

    reorder = (jnp.asarray(order)[:, None] == lax.broadcasted_iota(jnp.int32, (columns, columns), 1))
    ending = jnp.einsum("jn,jp->np", ending, reorder.astype(jnp.float32), precision=highest)
    ending = ending.reshape(groups, components, axial_rows, radial_rows, columns)
    upcoming = jnp.concatenate([start_states[1:], following[None]], axis=0)
    return ending - upcoming


def solution(mesh):
    placed = (P("seg", None, "ax", "rad", None), P("ax", None, None), P("seg"), P())
    return jax.shard_map(
        body,
        mesh=mesh,
        in_specs=placed,
        out_specs=P("seg", None, "ax", "rad", None),
        check_vma=False,
    )
```

```python
import functools
import math

import numpy as np
import jax
import jax.numpy as jnp
from jax import lax
from jax.experimental import pallas as pl
from jax.experimental.pallas import tpu as pltpu
from jax.sharding import PartitionSpec as P

STEPS = 2


highest = lax.Precision.HIGHEST
MESH_ID = pl.DeviceIdType.MESH


def passed_along(value, axis, steps):
    count = lax.axis_size(axis)
    pairs = [(source, (source + steps) % count) for source in range(count)]
    return lax.ppermute(value, axis, pairs)


def padded_2(array, sides, width):
    for axis, dim in sides:
        peers, length = (lax.axis_size(axis), array.shape[dim])
        up = [(i, (i + 1) % peers) for i in range(peers)]
        down = [(j, i) for i, j in up]
        last = lax.slice_in_dim(array, length - width, length, axis=dim)
        leading = lax.slice_in_dim(array, 0, width, axis=dim)
        before = lax.ppermute(last, axis, up)
        after = lax.ppermute(leading, axis, down)
        array = jnp.concatenate([before, array, after], axis=dim)
    return array


def exchange_kernel(axes, sizes, x_ref, o_ref, send_sem, recv_sem, local_sem):
    count = x_ref.shape[0]

    def place(index):
        coords = {}
        for axis, size in reversed(list(zip(axes, sizes))):
            coords[axis] = index % size
            index = index // size
        return coords

    me = 0
    for axis, size in zip(axes, sizes):
        me = me * size + lax.axis_index(axis)
    barrier = pltpu.get_barrier_semaphore()
    for step in range(1, count):
        pl.semaphore_signal(
            barrier, inc=1, device_id=place((me + step) % count), device_id_type=MESH_ID
        )
    pl.semaphore_wait(barrier, count - 1)
    local = pltpu.make_async_copy(x_ref.at[me], o_ref.at[me], local_sem)
    local.start()
    copies = []
    for step in range(1, count):
        hop = (step + 1) // 2 if step % 2 else count - step // 2
        peer = (me + hop) % count
        copy = pltpu.make_async_remote_copy(
            src_ref=x_ref.at[peer],
            dst_ref=o_ref.at[me],
            send_sem=send_sem.at[step - 1],
            recv_sem=recv_sem.at[step - 1],
            device_id=place(peer),
            device_id_type=MESH_ID,
        )
        copy.start()
        copies.append(copy)
    local.wait()
    for copy in copies:
        copy.wait()


def exchange(x, axes, collective_id):
    count = x.shape[0]
    sizes = tuple(lax.axis_size(axis) for axis in axes)
    return pl.pallas_call(
        functools.partial(exchange_kernel, axes, sizes),
        out_shape=jax.ShapeDtypeStruct(x.shape, x.dtype),
        in_specs=[pl.BlockSpec(memory_space=pl.ANY)],
        out_specs=pl.BlockSpec(memory_space=pl.ANY),
        scratch_shapes=[
            pltpu.SemaphoreType.DMA((count - 1,)),
            pltpu.SemaphoreType.DMA((count - 1,)),
            pltpu.SemaphoreType.DMA,
        ],
        compiler_params=pltpu.CompilerParams(
            collective_id=collective_id, has_side_effects=True
        ),
    )(x)


def mode_classes(ax_count, local_modes, classes):
    assert local_modes == 6 and classes == 8 and ax_count % 4 == 0
    slots = np.zeros((4, classes), np.int32)
    for d in range(4):
        given = [c for c in range(classes) if c // 2 != d]
        for index, c in enumerate(given):
            slots[d][c] = index
    class_modes = []
    for c in range(classes):
        modes = []
        for quad in range(ax_count // 4):
            for d in range(4):
                if d != c // 2:
                    modes.append((4 * quad + d) * local_modes + slots[d][c])
        class_modes.append(modes)
    class_modes = np.array(class_modes, np.int32)
    assert sorted(class_modes.reshape(-1).tolist()) == list(range(ax_count * local_modes))
    columns = np.stack([2 * class_modes, 2 * class_modes + 1], axis=-1).reshape(-1)
    return slots, columns


def fourier_tables(columns, kept_modes, order):
    modes_total = columns // 2
    row_index = jnp.asarray(order)[:, None]
    point_index = lax.broadcasted_iota(jnp.int32, (columns, columns), 1)
    mode_index = row_index // 2
    phase = (mode_index * point_index % columns).astype(jnp.float32) * (2.0 * math.pi / columns)
    even_rows = row_index % 2 == 0
    cosine = jnp.cos(phase)
    sine = jnp.sin(phase)
    root = math.sqrt(modes_total)
    synthesis = jnp.where(even_rows, cosine, sine) / root
    weights = jnp.where(mode_index == 0, 1.0, 2.0)
    analysis = jnp.where(even_rows, weights * cosine, 2.0 * sine) * (root / columns)
    analysis = jnp.where(mode_index < kept_modes, analysis, 0.0)
    return (synthesis, analysis)


def body(start_states, radial_inverse, offsets, mode_count):
    groups, components, axial_rows, radial_rows, columns = start_states.shape
    local_modes = radial_inverse.shape[0]
    ax_count = lax.axis_size("ax")
    seg_count = lax.axis_size("seg")
    rad_count = lax.axis_size("rad")
    classes = seg_count * rad_count
    radial_total = radial_rows * rad_count
    class_modes = columns // 2 // classes
    vectors = groups * components * axial_rows
    lanes = vectors * radial_rows
    slots, order = mode_classes(ax_count, local_modes, classes)
    ring = ("seg", "rad")

    me = lax.axis_index("seg") * rad_count + lax.axis_index("rad")
    own = jnp.asarray(slots)[lax.axis_index("ax") % 4, me]
    contribution = lax.dynamic_slice_in_dim(radial_inverse, own, 1, axis=0)
    gathered = lax.all_gather(contribution, "ax", axis=0, tiled=True)
    gathered = gathered.reshape(ax_count // 4, 4, radial_total, radial_total)
    slot = lax.broadcasted_iota(jnp.int32, (1, 3, 1, 1), 1)
    operators = jnp.where(slot < me // 2, gathered[:, 0:3], gathered[:, 1:4])
    operators = operators.reshape(class_modes, radial_total, radial_total)

    natural = np.arange(columns, dtype=np.int32)
    synthesis_first, _ = fourier_tables(columns, mode_count[0], natural)
    synthesis, analysis = fourier_tables(columns, mode_count[0], order)
    radius = (
        (lax.axis_index("rad") * radial_rows + jnp.arange(radial_rows)).astype(jnp.float32) + 0.5
    ) / radial_total
    profile = (1.0 - radius * radius).reshape(1, 1, 1, radial_rows, 1)
    following = passed_along(start_states[0], "seg", -1)
    current = start_states.reshape(lanes, columns)
    for step_index in range(STEPS):
        if step_index == 0:
            physical = jnp.dot(current, synthesis_first, precision=highest)
        else:
            physical = jnp.einsum("jn,jp->np", current, synthesis, precision=highest)
        physical = physical.reshape(groups, components, axial_rows, radial_rows, columns)
        padded = padded_2(physical, (("ax", 2),), 1)
        gradient = (padded[:, :, 2:] - padded[:, :, :-2]) * 20.0
        advecting = profile + padded[:, 2:3, 1:-1]
        forcing = physical - 0.02 * advecting * gradient
        forcing = forcing.reshape(lanes, columns)
        spectral = jnp.einsum("np,jp->jn", forcing, analysis, precision=highest)
        spectral = spectral.reshape(classes, 2 * class_modes, lanes)
        pencils = exchange(spectral, ring, 0)
        pencils = pencils.reshape(
            seg_count, rad_count, class_modes, 2 * vectors, radial_rows
        )
        pencils = jnp.transpose(pencils, (2, 0, 3, 1, 4)).reshape(
            class_modes, seg_count * 2 * vectors, radial_total
        )
        solved = jnp.einsum("mns,mrs->mnr", pencils, operators, precision=highest)
        solved = solved.reshape(class_modes, seg_count, 2 * vectors, rad_count, radial_rows)
        solved = jnp.transpose(solved, (1, 3, 0, 2, 4)).reshape(classes, 2 * class_modes, lanes)
        returned = exchange(solved, ring, 0)
        current = returned.reshape(columns, lanes)

    chunk = columns // ax_count
    dense = (ax_count, chunk * lanes // 128, 128)
    blocks = exchange(current.reshape(dense), ("ax",), 1)
    blocks = blocks.reshape(ax_count, chunk, groups, components, axial_rows, radial_rows)
    blocks = jnp.transpose(blocks, (1, 2, 3, 0, 4, 5)).reshape(
        chunk, groups, components, ax_count * axial_rows, radial_rows
    )
    shifted = [jnp.roll(blocks[:, member], offsets[member], axis=2) for member in range(groups)]
    blocks = jnp.stack(shifted, axis=1).reshape(
        chunk, groups, components, ax_count, axial_rows, radial_rows
    )
    blocks = jnp.transpose(blocks, (3, 0, 1, 2, 4, 5)).reshape(dense)
    ending = exchange(blocks, ("ax",), 1).reshape(columns, lanes)

    reorder = (jnp.asarray(order)[:, None] == lax.broadcasted_iota(jnp.int32, (columns, columns), 1))
    ending = jnp.einsum("jn,jp->np", ending, reorder.astype(jnp.float32), precision=highest)
    ending = ending.reshape(groups, components, axial_rows, radial_rows, columns)
    upcoming = jnp.concatenate([start_states[1:], following[None]], axis=0)
    return ending - upcoming


def solution(mesh):
    placed = (P("seg", None, "ax", "rad", None), P("ax", None, None), P("seg"), P())
    return jax.shard_map(
        body,
        mesh=mesh,
        in_specs=placed,
        out_specs=P("seg", None, "ax", "rad", None),
        check_vma=False,
    )
```

```python
import functools
import math

import numpy as np
import jax
import jax.numpy as jnp
from jax import lax
from jax.experimental import pallas as pl
from jax.experimental.pallas import tpu as pltpu
from jax.sharding import PartitionSpec as P

STEPS = 2


highest = lax.Precision.HIGHEST
MESH_ID = pl.DeviceIdType.MESH


def passed_along(value, axis, steps):
    count = lax.axis_size(axis)
    pairs = [(source, (source + steps) % count) for source in range(count)]
    return lax.ppermute(value, axis, pairs)


def halo_planes(array, axis, dim):
    peers, length = (lax.axis_size(axis), array.shape[dim])
    up = [(i, (i + 1) % peers) for i in range(peers)]
    down = [(j, i) for i, j in up]
    last = lax.slice_in_dim(array, length - 1, length, axis=dim)
    leading = lax.slice_in_dim(array, 0, 1, axis=dim)
    return lax.ppermute(last, axis, up), lax.ppermute(leading, axis, down)


def padded_2(array, sides, width):
    for axis, dim in sides:
        peers, length = (lax.axis_size(axis), array.shape[dim])
        up = [(i, (i + 1) % peers) for i in range(peers)]
        down = [(j, i) for i, j in up]
        last = lax.slice_in_dim(array, length - width, length, axis=dim)
        leading = lax.slice_in_dim(array, 0, width, axis=dim)
        before = lax.ppermute(last, axis, up)
        after = lax.ppermute(leading, axis, down)
        array = jnp.concatenate([before, array, after], axis=dim)
    return array


def exchange_kernel(axes, sizes, x_ref, o_ref, send_sem, recv_sem, local_sem):
    count = x_ref.shape[0]

    def place(index):
        coords = {}
        for axis, size in reversed(list(zip(axes, sizes))):
            coords[axis] = index % size
            index = index // size
        return coords

    me = 0
    for axis, size in zip(axes, sizes):
        me = me * size + lax.axis_index(axis)
    barrier = pltpu.get_barrier_semaphore()
    for step in range(1, count):
        pl.semaphore_signal(
            barrier, inc=1, device_id=place((me + step) % count), device_id_type=MESH_ID
        )
    pl.semaphore_wait(barrier, count - 1)
    local = pltpu.make_async_copy(x_ref.at[me], o_ref.at[me], local_sem)
    local.start()
    copies = []
    for step in range(1, count):
        hop = (step + 1) // 2 if step % 2 else count - step // 2
        peer = (me + hop) % count
        copy = pltpu.make_async_remote_copy(
            src_ref=x_ref.at[peer],
            dst_ref=o_ref.at[me],
            send_sem=send_sem.at[step - 1],
            recv_sem=recv_sem.at[step - 1],
            device_id=place(peer),
            device_id_type=MESH_ID,
        )
        copy.start()
        copies.append(copy)
    local.wait()
    for copy in copies:
        copy.wait()


def exchange(x, axes, collective_id):
    count = x.shape[0]
    sizes = tuple(lax.axis_size(axis) for axis in axes)
    return pl.pallas_call(
        functools.partial(exchange_kernel, axes, sizes),
        out_shape=jax.ShapeDtypeStruct(x.shape, x.dtype),
        in_specs=[pl.BlockSpec(memory_space=pl.ANY)],
        out_specs=pl.BlockSpec(memory_space=pl.ANY),
        scratch_shapes=[
            pltpu.SemaphoreType.DMA((count - 1,)),
            pltpu.SemaphoreType.DMA((count - 1,)),
            pltpu.SemaphoreType.DMA,
        ],
        compiler_params=pltpu.CompilerParams(
            collective_id=collective_id, has_side_effects=True
        ),
    )(x)


def mode_classes(ax_count, local_modes, classes):
    assert local_modes == 6 and classes == 8 and ax_count % 4 == 0
    slots = np.zeros((4, classes), np.int32)
    for d in range(4):
        given = [c for c in range(classes) if c // 2 != d]
        for index, c in enumerate(given):
            slots[d][c] = index
    class_modes = []
    for c in range(classes):
        modes = []
        for quad in range(ax_count // 4):
            for d in range(4):
                if d != c // 2:
                    modes.append((4 * quad + d) * local_modes + slots[d][c])
        class_modes.append(modes)
    class_modes = np.array(class_modes, np.int32)
    assert sorted(class_modes.reshape(-1).tolist()) == list(range(ax_count * local_modes))
    columns = np.stack([2 * class_modes, 2 * class_modes + 1], axis=-1).reshape(-1)
    return slots, columns


def fourier_tables(columns, kept_modes, order):
    modes_total = columns // 2
    row_index = jnp.asarray(order)[:, None]
    point_index = lax.broadcasted_iota(jnp.int32, (columns, columns), 1)
    mode_index = row_index // 2
    phase = (mode_index * point_index % columns).astype(jnp.float32) * (2.0 * math.pi / columns)
    even_rows = row_index % 2 == 0
    cosine = jnp.cos(phase)
    sine = jnp.sin(phase)
    root = math.sqrt(modes_total)
    synthesis = jnp.where(even_rows, cosine, sine) / root
    weights = jnp.where(mode_index == 0, 1.0, 2.0)
    analysis = jnp.where(even_rows, weights * cosine, 2.0 * sine) * (root / columns)
    analysis = jnp.where(mode_index < kept_modes, analysis, 0.0)
    return (synthesis, analysis)


def body(start_states, radial_inverse, offsets, mode_count):
    groups, components, axial_rows, radial_rows, columns = start_states.shape
    local_modes = radial_inverse.shape[0]
    ax_count = lax.axis_size("ax")
    seg_count = lax.axis_size("seg")
    rad_count = lax.axis_size("rad")
    classes = seg_count * rad_count
    radial_total = radial_rows * rad_count
    class_modes = columns // 2 // classes
    vectors = groups * components * axial_rows
    lanes = vectors * radial_rows
    slots, order = mode_classes(ax_count, local_modes, classes)
    ring = ("seg", "rad")

    me = lax.axis_index("seg") * rad_count + lax.axis_index("rad")
    own = jnp.asarray(slots)[lax.axis_index("ax") % 4, me]
    contribution = lax.dynamic_slice_in_dim(radial_inverse, own, 1, axis=0)
    gathered = lax.all_gather(contribution, "ax", axis=0, tiled=True)
    gathered = gathered.reshape(ax_count // 4, 4, radial_total, radial_total)
    slot = lax.broadcasted_iota(jnp.int32, (1, 3, 1, 1), 1)
    operators = jnp.where(slot < me // 2, gathered[:, 0:3], gathered[:, 1:4])
    operators = operators.reshape(class_modes, radial_total, radial_total)

    natural = np.arange(columns, dtype=np.int32)
    synthesis_first, _ = fourier_tables(columns, mode_count[0], natural)
    synthesis, analysis = fourier_tables(columns, mode_count[0], order)
    radius = (
        (lax.axis_index("rad") * radial_rows + jnp.arange(radial_rows)).astype(jnp.float32) + 0.5
    ) / radial_total
    profile = (1.0 - radius * radius).reshape(1, 1, 1, radial_rows, 1)
    following = passed_along(start_states[0], "seg", -1)
    current = start_states.reshape(lanes, columns)
    for step_index in range(STEPS):
        if step_index == 0:
            before, after = halo_planes(start_states, "ax", 2)
            edges = jnp.concatenate([before, after], axis=2)
            edges = jnp.dot(
                edges.reshape(-1, columns), synthesis_first, precision=highest
            ).reshape(groups, components, 2, radial_rows, columns)
            physical = jnp.dot(current, synthesis_first, precision=highest)
            physical = physical.reshape(groups, components, axial_rows, radial_rows, columns)
            padded = jnp.concatenate([edges[:, :, :1], physical, edges[:, :, 1:]], axis=2)
        else:
            physical = jnp.einsum("jn,jp->np", current, synthesis, precision=highest)
            physical = physical.reshape(groups, components, axial_rows, radial_rows, columns)
            padded = padded_2(physical, (("ax", 2),), 1)
        gradient = (padded[:, :, 2:] - padded[:, :, :-2]) * 20.0
        advecting = profile + padded[:, 2:3, 1:-1]
        forcing = physical - 0.02 * advecting * gradient
        forcing = forcing.reshape(lanes, columns)
        spectral = jnp.einsum("np,jp->jn", forcing, analysis, precision=highest)
        spectral = spectral.reshape(classes, 2 * class_modes, lanes)
        pencils = exchange(spectral, ring, 0)
        pencils = pencils.reshape(
            seg_count, rad_count, class_modes, 2 * vectors, radial_rows
        )
        pencils = jnp.transpose(pencils, (2, 0, 3, 1, 4)).reshape(
            class_modes, seg_count * 2 * vectors, radial_total
        )
        solved = jnp.einsum("mns,mrs->mnr", pencils, operators, precision=highest)
        solved = solved.reshape(class_modes, seg_count, 2 * vectors, rad_count, radial_rows)
        solved = jnp.transpose(solved, (1, 3, 0, 2, 4)).reshape(classes, 2 * class_modes, lanes)
        returned = exchange(solved, ring, 0)
        current = returned.reshape(columns, lanes)

    chunk = columns // ax_count
    dense = (ax_count, chunk * lanes // 128, 128)
    blocks = exchange(current.reshape(dense), ("ax",), 1)
    blocks = blocks.reshape(ax_count, chunk, groups, components, axial_rows, radial_rows)
    blocks = jnp.transpose(blocks, (1, 2, 3, 0, 4, 5)).reshape(
        chunk, groups, components, ax_count * axial_rows, radial_rows
    )
    shifted = [jnp.roll(blocks[:, member], offsets[member], axis=2) for member in range(groups)]
    blocks = jnp.stack(shifted, axis=1).reshape(
        chunk, groups, components, ax_count, axial_rows, radial_rows
    )
    blocks = jnp.transpose(blocks, (3, 0, 1, 2, 4, 5)).reshape(dense)
    ending = exchange(blocks, ("ax",), 1).reshape(columns, lanes)

    reorder = (jnp.asarray(order)[:, None] == lax.broadcasted_iota(jnp.int32, (columns, columns), 1))
    ending = jnp.einsum("jn,jp->np", ending, reorder.astype(jnp.float32), precision=highest)
    ending = ending.reshape(groups, components, axial_rows, radial_rows, columns)
    upcoming = jnp.concatenate([start_states[1:], following[None]], axis=0)
    return ending - upcoming


def solution(mesh):
    placed = (P("seg", None, "ax", "rad", None), P("ax", None, None), P("seg"), P())
    return jax.shard_map(
        body,
        mesh=mesh,
        in_specs=placed,
        out_specs=P("seg", None, "ax", "rad", None),
        check_vma=False,
    )
```

```python
import functools
import math

import numpy as np
import jax
import jax.numpy as jnp
from jax import lax
from jax.experimental import pallas as pl
from jax.experimental.pallas import tpu as pltpu
from jax.sharding import PartitionSpec as P

STEPS = 2


highest = lax.Precision.HIGHEST
MESH_ID = pl.DeviceIdType.MESH


def passed_along(value, axis, steps):
    count = lax.axis_size(axis)
    pairs = [(source, (source + steps) % count) for source in range(count)]
    return lax.ppermute(value, axis, pairs)


def halo_planes(array, axis, dim):
    peers, length = (lax.axis_size(axis), array.shape[dim])
    up = [(i, (i + 1) % peers) for i in range(peers)]
    down = [(j, i) for i, j in up]
    last = lax.slice_in_dim(array, length - 1, length, axis=dim)
    leading = lax.slice_in_dim(array, 0, 1, axis=dim)
    return lax.ppermute(last, axis, up), lax.ppermute(leading, axis, down)


def padded_2(array, sides, width):
    for axis, dim in sides:
        peers, length = (lax.axis_size(axis), array.shape[dim])
        up = [(i, (i + 1) % peers) for i in range(peers)]
        down = [(j, i) for i, j in up]
        last = lax.slice_in_dim(array, length - width, length, axis=dim)
        leading = lax.slice_in_dim(array, 0, width, axis=dim)
        before = lax.ppermute(last, axis, up)
        after = lax.ppermute(leading, axis, down)
        array = jnp.concatenate([before, array, after], axis=dim)
    return array


def exchange_kernel(axes, sizes, x_ref, o_ref, send_sem, recv_sem, local_sem):
    count = x_ref.shape[0]

    def place(index):
        coords = {}
        for axis, size in reversed(list(zip(axes, sizes))):
            coords[axis] = index % size
            index = index // size
        return coords

    me = 0
    for axis, size in zip(axes, sizes):
        me = me * size + lax.axis_index(axis)
    barrier = pltpu.get_barrier_semaphore()
    for step in range(1, count):
        pl.semaphore_signal(
            barrier, inc=1, device_id=place((me + step) % count), device_id_type=MESH_ID
        )
    pl.semaphore_wait(barrier, count - 1)
    local = pltpu.make_async_copy(x_ref.at[me], o_ref.at[me], local_sem)
    local.start()
    copies = []
    for step in range(1, count):
        hop = (step + 1) // 2 if step % 2 else count - step // 2
        peer = (me + hop) % count
        copy = pltpu.make_async_remote_copy(
            src_ref=x_ref.at[peer],
            dst_ref=o_ref.at[me],
            send_sem=send_sem.at[step - 1],
            recv_sem=recv_sem.at[step - 1],
            device_id=place(peer),
            device_id_type=MESH_ID,
        )
        copy.start()
        copies.append(copy)
    local.wait()
    for copy in copies:
        copy.wait()


def exchange(x, axes, collective_id):
    count = x.shape[0]
    sizes = tuple(lax.axis_size(axis) for axis in axes)
    return pl.pallas_call(
        functools.partial(exchange_kernel, axes, sizes),
        out_shape=jax.ShapeDtypeStruct(x.shape, x.dtype),
        in_specs=[pl.BlockSpec(memory_space=pl.ANY)],
        out_specs=pl.BlockSpec(memory_space=pl.ANY),
        scratch_shapes=[
            pltpu.SemaphoreType.DMA((count - 1,)),
            pltpu.SemaphoreType.DMA((count - 1,)),
            pltpu.SemaphoreType.DMA,
        ],
        compiler_params=pltpu.CompilerParams(
            collective_id=collective_id, has_side_effects=True
        ),
    )(x)


def mode_classes(ax_count, local_modes, classes):
    assert local_modes == 6 and classes == 8 and ax_count % 4 == 0
    slots = np.zeros((4, classes), np.int32)
    for d in range(4):
        given = [c for c in range(classes) if c // 2 != d]
        for index, c in enumerate(given):
            slots[d][c] = index
    class_modes = []
    for c in range(classes):
        modes = []
        for quad in range(ax_count // 4):
            for d in range(4):
                if d != c // 2:
                    modes.append((4 * quad + d) * local_modes + slots[d][c])
        class_modes.append(modes)
    class_modes = np.array(class_modes, np.int32)
    assert sorted(class_modes.reshape(-1).tolist()) == list(range(ax_count * local_modes))
    columns = np.stack([2 * class_modes, 2 * class_modes + 1], axis=-1).reshape(-1)
    return slots, columns


def fourier_tables(columns, kept_modes, order):
    modes_total = columns // 2
    row_index = jnp.asarray(order)[:, None]
    point_index = lax.broadcasted_iota(jnp.int32, (columns, columns), 1)
    mode_index = row_index // 2
    phase = (mode_index * point_index % columns).astype(jnp.float32) * (2.0 * math.pi / columns)
    even_rows = row_index % 2 == 0
    cosine = jnp.cos(phase)
    sine = jnp.sin(phase)
    root = math.sqrt(modes_total)
    synthesis = jnp.where(even_rows, cosine, sine) / root
    weights = jnp.where(mode_index == 0, 1.0, 2.0)
    analysis = jnp.where(even_rows, weights * cosine, 2.0 * sine) * (root / columns)
    analysis = jnp.where(mode_index < kept_modes, analysis, 0.0)
    return (synthesis, analysis)


def body(start_states, radial_inverse, offsets, mode_count):
    groups, components, axial_rows, radial_rows, columns = start_states.shape
    local_modes = radial_inverse.shape[0]
    ax_count = lax.axis_size("ax")
    seg_count = lax.axis_size("seg")
    rad_count = lax.axis_size("rad")
    classes = seg_count * rad_count
    radial_total = radial_rows * rad_count
    class_modes = columns // 2 // classes
    vectors = groups * components * axial_rows
    lanes = vectors * radial_rows
    slots, order = mode_classes(ax_count, local_modes, classes)
    ring = ("seg", "rad")

    me = lax.axis_index("seg") * rad_count + lax.axis_index("rad")
    own = jnp.asarray(slots)[lax.axis_index("ax") % 4, me]
    contribution = lax.dynamic_slice_in_dim(radial_inverse, own, 1, axis=0)
    gathered = lax.all_gather(contribution, "ax", axis=0, tiled=True)
    gathered = gathered.reshape(ax_count // 4, 4, radial_total, radial_total)
    slot = lax.broadcasted_iota(jnp.int32, (1, 3, 1, 1), 1)
    operators = jnp.where(slot < me // 2, gathered[:, 0:3], gathered[:, 1:4])
    operators = operators.reshape(class_modes, radial_total, radial_total)

    natural = np.arange(columns, dtype=np.int32)
    synthesis_first, _ = fourier_tables(columns, mode_count[0], natural)
    synthesis, analysis = fourier_tables(columns, mode_count[0], order)
    radius = (
        (lax.axis_index("rad") * radial_rows + jnp.arange(radial_rows)).astype(jnp.float32) + 0.5
    ) / radial_total
    profile = (1.0 - radius * radius).reshape(1, 1, 1, radial_rows, 1)
    following = passed_along(start_states[0], "seg", -1)
    current = start_states.reshape(lanes, columns)
    for step_index in range(STEPS):
        if step_index == 0:
            before, after = halo_planes(start_states, "ax", 2)
            edges = jnp.concatenate([before, after], axis=2)
            edges = jnp.dot(
                edges.reshape(-1, columns), synthesis_first, precision=highest
            ).reshape(groups, components, 2, radial_rows, columns)
            physical = jnp.dot(current, synthesis_first, precision=highest)
            physical = physical.reshape(groups, components, axial_rows, radial_rows, columns)
            padded = jnp.concatenate([edges[:, :, :1], physical, edges[:, :, 1:]], axis=2)
        else:
            planes = current.reshape(columns, groups * components, axial_rows, radial_rows)
            before, after = halo_planes(planes, "ax", 2)
            edges = jnp.concatenate([before, after], axis=2)
            edges = jnp.einsum(
                "jn,jp->np", edges.reshape(columns, -1), synthesis, precision=highest
            ).reshape(groups, components, 2, radial_rows, columns)
            physical = jnp.einsum("jn,jp->np", current, synthesis, precision=highest)
            physical = physical.reshape(groups, components, axial_rows, radial_rows, columns)
            padded = jnp.concatenate([edges[:, :, :1], physical, edges[:, :, 1:]], axis=2)
        gradient = (padded[:, :, 2:] - padded[:, :, :-2]) * 20.0
        advecting = profile + padded[:, 2:3, 1:-1]
        forcing = physical - 0.02 * advecting * gradient
        forcing = forcing.reshape(lanes, columns)
        spectral = jnp.einsum("np,jp->jn", forcing, analysis, precision=highest)
        spectral = spectral.reshape(classes, 2 * class_modes, lanes)
        pencils = exchange(spectral, ring, 0)
        pencils = pencils.reshape(
            seg_count, rad_count, class_modes, 2 * vectors, radial_rows
        )
        pencils = jnp.transpose(pencils, (2, 0, 3, 1, 4)).reshape(
            class_modes, seg_count * 2 * vectors, radial_total
        )
        solved = jnp.einsum("mns,mrs->mnr", pencils, operators, precision=highest)
        solved = solved.reshape(class_modes, seg_count, 2 * vectors, rad_count, radial_rows)
        solved = jnp.transpose(solved, (1, 3, 0, 2, 4)).reshape(classes, 2 * class_modes, lanes)
        returned = exchange(solved, ring, 0)
        current = returned.reshape(columns, lanes)

    chunk = columns // ax_count
    dense = (ax_count, chunk * lanes // 128, 128)
    blocks = exchange(current.reshape(dense), ("ax",), 1)
    blocks = blocks.reshape(ax_count, chunk, groups, components, axial_rows, radial_rows)
    blocks = jnp.transpose(blocks, (1, 2, 3, 0, 4, 5)).reshape(
        chunk, groups, components, ax_count * axial_rows, radial_rows
    )
    shifted = [jnp.roll(blocks[:, member], offsets[member], axis=2) for member in range(groups)]
    blocks = jnp.stack(shifted, axis=1).reshape(
        chunk, groups, components, ax_count, axial_rows, radial_rows
    )
    blocks = jnp.transpose(blocks, (3, 0, 1, 2, 4, 5)).reshape(dense)
    ending = exchange(blocks, ("ax",), 1).reshape(columns, lanes)

    reorder = (jnp.asarray(order)[:, None] == lax.broadcasted_iota(jnp.int32, (columns, columns), 1))
    ending = jnp.einsum("jn,jp->np", ending, reorder.astype(jnp.float32), precision=highest)
    ending = ending.reshape(groups, components, axial_rows, radial_rows, columns)
    upcoming = jnp.concatenate([start_states[1:], following[None]], axis=0)
    return ending - upcoming


def solution(mesh):
    placed = (P("seg", None, "ax", "rad", None), P("ax", None, None), P("seg"), P())
    return jax.shard_map(
        body,
        mesh=mesh,
        in_specs=placed,
        out_specs=P("seg", None, "ax", "rad", None),
        check_vma=False,
    )
```

```python
import functools
import math

import numpy as np
import jax
import jax.numpy as jnp
from jax import lax
from jax.experimental import pallas as pl
from jax.experimental.pallas import tpu as pltpu
from jax.sharding import PartitionSpec as P

STEPS = 2


highest = lax.Precision.HIGHEST
MESH_ID = pl.DeviceIdType.MESH


def passed_along(value, axis, steps):
    count = lax.axis_size(axis)
    pairs = [(source, (source + steps) % count) for source in range(count)]
    return lax.ppermute(value, axis, pairs)


def padded_2(array, sides, width):
    for axis, dim in sides:
        peers, length = (lax.axis_size(axis), array.shape[dim])
        up = [(i, (i + 1) % peers) for i in range(peers)]
        down = [(j, i) for i, j in up]
        last = lax.slice_in_dim(array, length - width, length, axis=dim)
        leading = lax.slice_in_dim(array, 0, width, axis=dim)
        before = lax.ppermute(last, axis, up)
        after = lax.ppermute(leading, axis, down)
        array = jnp.concatenate([before, array, after], axis=dim)
    return array


def exchange_kernel(axes, sizes, x_ref, o_ref, send_sem, recv_sem, local_sem):
    count = x_ref.shape[0]

    def place(index):
        coords = {}
        for axis, size in reversed(list(zip(axes, sizes))):
            coords[axis] = index % size
            index = index // size
        return coords

    me = 0
    for axis, size in zip(axes, sizes):
        me = me * size + lax.axis_index(axis)
    barrier = pltpu.get_barrier_semaphore()
    for step in range(1, count):
        pl.semaphore_signal(
            barrier, inc=1, device_id=place((me + step) % count), device_id_type=MESH_ID
        )
    pl.semaphore_wait(barrier, count - 1)
    copies = []
    for step in range(1, count):
        hop = (step + 1) // 2 if step % 2 else count - step // 2
        peer = (me + hop) % count
        copy = pltpu.make_async_remote_copy(
            src_ref=x_ref.at[peer],
            dst_ref=o_ref.at[me],
            send_sem=send_sem.at[step - 1],
            recv_sem=recv_sem.at[step - 1],
            device_id=place(peer),
            device_id_type=MESH_ID,
        )
        copy.start()
        copies.append(copy)
    local = pltpu.make_async_copy(x_ref.at[me], o_ref.at[me], local_sem)
    local.start()
    local.wait()
    for copy in copies:
        copy.wait()


def exchange(x, axes, collective_id):
    count = x.shape[0]
    sizes = tuple(lax.axis_size(axis) for axis in axes)
    return pl.pallas_call(
        functools.partial(exchange_kernel, axes, sizes),
        out_shape=jax.ShapeDtypeStruct(x.shape, x.dtype),
        in_specs=[pl.BlockSpec(memory_space=pl.ANY)],
        out_specs=pl.BlockSpec(memory_space=pl.ANY),
        scratch_shapes=[
            pltpu.SemaphoreType.DMA((count - 1,)),
            pltpu.SemaphoreType.DMA((count - 1,)),
            pltpu.SemaphoreType.DMA,
        ],
        compiler_params=pltpu.CompilerParams(
            collective_id=collective_id, has_side_effects=True
        ),
    )(x)


def mode_classes(ax_count, local_modes, classes):
    assert local_modes == 6 and classes == 8 and ax_count % 4 == 0
    slots = np.zeros((4, classes), np.int32)
    for d in range(4):
        given = [c for c in range(classes) if c // 2 != d]
        for index, c in enumerate(given):
            slots[d][c] = index
    class_modes = []
    for c in range(classes):
        modes = []
        for quad in range(ax_count // 4):
            for d in range(4):
                if d != c // 2:
                    modes.append((4 * quad + d) * local_modes + slots[d][c])
        class_modes.append(modes)
    class_modes = np.array(class_modes, np.int32)
    assert sorted(class_modes.reshape(-1).tolist()) == list(range(ax_count * local_modes))
    columns = np.stack([2 * class_modes, 2 * class_modes + 1], axis=-1).reshape(-1)
    return slots, columns


def fourier_tables(columns, kept_modes, order):
    modes_total = columns // 2
    row_index = jnp.asarray(order)[:, None]
    point_index = lax.broadcasted_iota(jnp.int32, (columns, columns), 1)
    mode_index = row_index // 2
    phase = (mode_index * point_index % columns).astype(jnp.float32) * (2.0 * math.pi / columns)
    even_rows = row_index % 2 == 0
    cosine = jnp.cos(phase)
    sine = jnp.sin(phase)
    root = math.sqrt(modes_total)
    synthesis = jnp.where(even_rows, cosine, sine) / root
    weights = jnp.where(mode_index == 0, 1.0, 2.0)
    analysis = jnp.where(even_rows, weights * cosine, 2.0 * sine) * (root / columns)
    analysis = jnp.where(mode_index < kept_modes, analysis, 0.0)
    return (synthesis, analysis)


def body(start_states, radial_inverse, offsets, mode_count):
    groups, components, axial_rows, radial_rows, columns = start_states.shape
    local_modes = radial_inverse.shape[0]
    ax_count = lax.axis_size("ax")
    seg_count = lax.axis_size("seg")
    rad_count = lax.axis_size("rad")
    classes = seg_count * rad_count
    radial_total = radial_rows * rad_count
    class_modes = columns // 2 // classes
    vectors = groups * components * axial_rows
    lanes = vectors * radial_rows
    slots, order = mode_classes(ax_count, local_modes, classes)
    ring = ("seg", "rad")

    me = lax.axis_index("seg") * rad_count + lax.axis_index("rad")
    own = jnp.asarray(slots)[lax.axis_index("ax") % 4, me]
    contribution = lax.dynamic_slice_in_dim(radial_inverse, own, 1, axis=0)
    gathered = lax.all_gather(contribution, "ax", axis=0, tiled=True)
    gathered = gathered.reshape(ax_count // 4, 4, radial_total, radial_total)
    slot = lax.broadcasted_iota(jnp.int32, (1, 3, 1, 1), 1)
    operators = jnp.where(slot < me // 2, gathered[:, 0:3], gathered[:, 1:4])
    operators = operators.reshape(class_modes, radial_total, radial_total)

    natural = np.arange(columns, dtype=np.int32)
    synthesis_first, _ = fourier_tables(columns, mode_count[0], natural)
    synthesis, analysis = fourier_tables(columns, mode_count[0], order)
    radius = (
        (lax.axis_index("rad") * radial_rows + jnp.arange(radial_rows)).astype(jnp.float32) + 0.5
    ) / radial_total
    profile = (1.0 - radius * radius).reshape(1, 1, 1, radial_rows, 1)
    following = passed_along(start_states[0], "seg", -1)
    current = start_states.reshape(lanes, columns)
    for step_index in range(STEPS):
        if step_index == 0:
            physical = jnp.dot(current, synthesis_first, precision=highest)
        else:
            physical = jnp.einsum("jn,jp->np", current, synthesis, precision=highest)
        physical = physical.reshape(groups, components, axial_rows, radial_rows, columns)
        padded = padded_2(physical, (("ax", 2),), 1)
        gradient = (padded[:, :, 2:] - padded[:, :, :-2]) * 20.0
        advecting = profile + padded[:, 2:3, 1:-1]
        forcing = physical - 0.02 * advecting * gradient
        forcing = forcing.reshape(lanes, columns)
        spectral = jnp.einsum("np,jp->jn", forcing, analysis, precision=highest)
        spectral = spectral.reshape(classes, 2 * class_modes, lanes)
        pencils = exchange(spectral, ring, 0)
        pencils = pencils.reshape(
            seg_count, rad_count, class_modes, 2 * vectors, radial_rows
        )
        pencils = jnp.transpose(pencils, (2, 0, 3, 1, 4)).reshape(
            class_modes, seg_count * 2 * vectors, radial_total
        )
        solved = jnp.einsum("mns,mrs->mnr", pencils, operators, precision=highest)
        solved = solved.reshape(class_modes, seg_count, 2 * vectors, rad_count, radial_rows)
        solved = jnp.transpose(solved, (1, 3, 0, 2, 4)).reshape(classes, 2 * class_modes, lanes)
        returned = exchange(solved, ring, 0)
        current = returned.reshape(columns, lanes)

    chunk = columns // ax_count
    dense = (ax_count, chunk * lanes // 128, 128)
    blocks = exchange(current.reshape(dense), ("ax",), 1)
    blocks = blocks.reshape(ax_count, chunk, groups, components, axial_rows, radial_rows)
    blocks = jnp.transpose(blocks, (1, 2, 3, 0, 4, 5)).reshape(
        chunk, groups, components, ax_count * axial_rows, radial_rows
    )
    shifted = [jnp.roll(blocks[:, member], offsets[member], axis=2) for member in range(groups)]
    blocks = jnp.stack(shifted, axis=1).reshape(
        chunk, groups, components, ax_count, axial_rows, radial_rows
    )
    blocks = jnp.transpose(blocks, (3, 0, 1, 2, 4, 5)).reshape(dense)
    ending = exchange(blocks, ("ax",), 1).reshape(columns, lanes)

    reorder = (jnp.asarray(order)[:, None] == lax.broadcasted_iota(jnp.int32, (columns, columns), 1))
    ending = jnp.einsum("jn,jp->np", ending, reorder.astype(jnp.float32), precision=highest)
    ending = ending.reshape(groups, components, axial_rows, radial_rows, columns)
    upcoming = jnp.concatenate([start_states[1:], following[None]], axis=0)
    return ending - upcoming


def solution(mesh):
    placed = (P("seg", None, "ax", "rad", None), P("ax", None, None), P("seg"), P())
    return jax.shard_map(
        body,
        mesh=mesh,
        in_specs=placed,
        out_specs=P("seg", None, "ax", "rad", None),
        check_vma=False,
    )
```

```python
import functools
import math

import numpy as np
import jax
import jax.numpy as jnp
from jax import lax
from jax.experimental import pallas as pl
from jax.experimental.pallas import tpu as pltpu
from jax.sharding import PartitionSpec as P

STEPS = 2


highest = lax.Precision.HIGHEST
MESH_ID = pl.DeviceIdType.MESH


def passed_along(value, axis, steps):
    count = lax.axis_size(axis)
    pairs = [(source, (source + steps) % count) for source in range(count)]
    return lax.ppermute(value, axis, pairs)


def padded_2(array, sides, width):
    for axis, dim in sides:
        peers, length = (lax.axis_size(axis), array.shape[dim])
        up = [(i, (i + 1) % peers) for i in range(peers)]
        down = [(j, i) for i, j in up]
        last = lax.slice_in_dim(array, length - width, length, axis=dim)
        leading = lax.slice_in_dim(array, 0, width, axis=dim)
        before = lax.ppermute(last, axis, up)
        after = lax.ppermute(leading, axis, down)
        array = jnp.concatenate([before, array, after], axis=dim)
    return array


def exchange_kernel(axes, sizes, x_ref, o_ref, send_sem, recv_sem, local_sem):
    count = x_ref.shape[0]

    def place(index):
        coords = {}
        for axis, size in reversed(list(zip(axes, sizes))):
            coords[axis] = index % size
            index = index // size
        return coords

    me = 0
    for axis, size in zip(axes, sizes):
        me = me * size + lax.axis_index(axis)
    barrier = pltpu.get_barrier_semaphore()
    for step in range(1, count):
        pl.semaphore_signal(
            barrier, inc=1, device_id=place((me + step) % count), device_id_type=MESH_ID
        )
    pl.semaphore_wait(barrier, count - 1)
    copies = []
    for step in range(1, count):
        hop = (step + 1) // 2 if step % 2 else count - step // 2
        peer = (me + hop) % count
        copy = pltpu.make_async_remote_copy(
            src_ref=x_ref.at[peer],
            dst_ref=o_ref.at[me],
            send_sem=send_sem.at[step - 1],
            recv_sem=recv_sem.at[step - 1],
            device_id=place(peer),
            device_id_type=MESH_ID,
        )
        copy.start()
        copies.append(copy)
    local = pltpu.make_async_copy(x_ref.at[me], o_ref.at[me], local_sem)
    local.start()
    local.wait()
    for copy in copies:
        copy.wait()


def exchange(x, axes, collective_id):
    count = x.shape[0]
    sizes = tuple(lax.axis_size(axis) for axis in axes)
    return pl.pallas_call(
        functools.partial(exchange_kernel, axes, sizes),
        out_shape=jax.ShapeDtypeStruct(x.shape, x.dtype),
        in_specs=[pl.BlockSpec(memory_space=pl.ANY)],
        out_specs=pl.BlockSpec(memory_space=pl.ANY),
        scratch_shapes=[
            pltpu.SemaphoreType.DMA((count - 1,)),
            pltpu.SemaphoreType.DMA((count - 1,)),
            pltpu.SemaphoreType.DMA,
        ],
        compiler_params=pltpu.CompilerParams(
            collective_id=collective_id, has_side_effects=True
        ),
    )(x)


def mode_classes(ax_count, local_modes, classes):
    assert local_modes == 6 and classes == 8 and ax_count % 4 == 0
    slots = np.zeros((4, classes), np.int32)
    for d in range(4):
        given = [c for c in range(classes) if c // 2 != d]
        for index, c in enumerate(given):
            slots[d][c] = index
    class_modes = []
    for c in range(classes):
        modes = []
        for quad in range(ax_count // 4):
            for d in range(4):
                if d != c // 2:
                    modes.append((4 * quad + d) * local_modes + slots[d][c])
        class_modes.append(modes)
    class_modes = np.array(class_modes, np.int32)
    assert sorted(class_modes.reshape(-1).tolist()) == list(range(ax_count * local_modes))
    columns = np.stack([2 * class_modes, 2 * class_modes + 1], axis=-1).reshape(-1)
    return slots, columns


def fourier_tables(columns, kept_modes, order):
    modes_total = columns // 2
    row_index = jnp.asarray(order)[:, None]
    point_index = lax.broadcasted_iota(jnp.int32, (columns, columns), 1)
    mode_index = row_index // 2
    phase = (mode_index * point_index % columns).astype(jnp.float32) * (2.0 * math.pi / columns)
    even_rows = row_index % 2 == 0
    cosine = jnp.cos(phase)
    sine = jnp.sin(phase)
    root = math.sqrt(modes_total)
    synthesis = jnp.where(even_rows, cosine, sine) / root
    weights = jnp.where(mode_index == 0, 1.0, 2.0)
    analysis = jnp.where(even_rows, weights * cosine, 2.0 * sine) * (root / columns)
    analysis = jnp.where(mode_index < kept_modes, analysis, 0.0)
    return (synthesis, analysis)


def body(start_states, radial_inverse, offsets, mode_count):
    groups, components, axial_rows, radial_rows, columns = start_states.shape
    local_modes = radial_inverse.shape[0]
    ax_count = lax.axis_size("ax")
    seg_count = lax.axis_size("seg")
    rad_count = lax.axis_size("rad")
    classes = seg_count * rad_count
    radial_total = radial_rows * rad_count
    class_modes = columns // 2 // classes
    vectors = groups * components * axial_rows
    lanes = vectors * radial_rows
    slots, order = mode_classes(ax_count, local_modes, classes)
    ring = ("seg", "rad")

    me = lax.axis_index("seg") * rad_count + lax.axis_index("rad")
    own = jnp.asarray(slots)[lax.axis_index("ax") % 4, me]
    contribution = lax.dynamic_slice_in_dim(radial_inverse, own, 1, axis=0)
    gathered = lax.all_gather(contribution, "ax", axis=0, tiled=True)
    gathered = gathered.reshape(ax_count // 4, 4, radial_total, radial_total)
    slot = lax.broadcasted_iota(jnp.int32, (1, 3, 1, 1), 1)
    operators = jnp.where(slot < me // 2, gathered[:, 0:3], gathered[:, 1:4])
    operators = operators.reshape(class_modes, radial_total, radial_total)

    natural = np.arange(columns, dtype=np.int32)
    synthesis_first, _ = fourier_tables(columns, mode_count[0], natural)
    synthesis, analysis = fourier_tables(columns, mode_count[0], order)
    radius = (
        (lax.axis_index("rad") * radial_rows + jnp.arange(radial_rows)).astype(jnp.float32) + 0.5
    ) / radial_total
    profile = (1.0 - radius * radius).reshape(1, 1, 1, radial_rows, 1)
    following = passed_along(start_states[0], "seg", -1)
    current = start_states.reshape(lanes, columns)
    for step_index in range(STEPS):
        if step_index == 0:
            physical = jnp.dot(current, synthesis_first, precision=highest)
        else:
            physical = jnp.einsum("jn,jp->np", current, synthesis, precision=highest)
        physical = physical.reshape(groups, components, axial_rows, radial_rows, columns)
        padded = padded_2(physical, (("ax", 2),), 1)
        gradient = (padded[:, :, 2:] - padded[:, :, :-2]) * 20.0
        advecting = profile + padded[:, 2:3, 1:-1]
        forcing = physical - 0.02 * advecting * gradient
        forcing = forcing.reshape(lanes, columns)
        spectral = jnp.einsum("np,jp->jn", forcing, analysis, precision=highest)
        spectral = spectral.reshape(classes, 2 * class_modes, lanes)
        pencils = exchange(spectral, ring, 0)
        pencils = pencils.reshape(
            seg_count, rad_count, class_modes, 2 * vectors, radial_rows
        )
        blocks = operators.reshape(class_modes, radial_total, rad_count, radial_rows)
        solved = sum(
            jnp.einsum(
                "gmns,mrs->gmnr", pencils[:, q], blocks[:, :, q], precision=highest
            )
            for q in range(rad_count)
        )
        solved = solved.reshape(seg_count, class_modes, 2 * vectors, rad_count, radial_rows)
        solved = jnp.transpose(solved, (0, 3, 1, 2, 4)).reshape(classes, 2 * class_modes, lanes)
        returned = exchange(solved, ring, 0)
        current = returned.reshape(columns, lanes)

    chunk = columns // ax_count
    dense = (ax_count, chunk * lanes // 128, 128)
    blocks = exchange(current.reshape(dense), ("ax",), 1)
    blocks = blocks.reshape(ax_count, chunk, groups, components, axial_rows, radial_rows)
    blocks = jnp.transpose(blocks, (1, 2, 3, 0, 4, 5)).reshape(
        chunk, groups, components, ax_count * axial_rows, radial_rows
    )
    shifted = [jnp.roll(blocks[:, member], offsets[member], axis=2) for member in range(groups)]
    blocks = jnp.stack(shifted, axis=1).reshape(
        chunk, groups, components, ax_count, axial_rows, radial_rows
    )
    blocks = jnp.transpose(blocks, (3, 0, 1, 2, 4, 5)).reshape(dense)
    ending = exchange(blocks, ("ax",), 1).reshape(columns, lanes)

    reorder = (jnp.asarray(order)[:, None] == lax.broadcasted_iota(jnp.int32, (columns, columns), 1))
    ending = jnp.einsum("jn,jp->np", ending, reorder.astype(jnp.float32), precision=highest)
    ending = ending.reshape(groups, components, axial_rows, radial_rows, columns)
    upcoming = jnp.concatenate([start_states[1:], following[None]], axis=0)
    return ending - upcoming


def solution(mesh):
    placed = (P("seg", None, "ax", "rad", None), P("ax", None, None), P("seg"), P())
    return jax.shard_map(
        body,
        mesh=mesh,
        in_specs=placed,
        out_specs=P("seg", None, "ax", "rad", None),
        check_vma=False,
    )
```

```python
import functools
import math

import numpy as np
import jax
import jax.numpy as jnp
from jax import lax
from jax.experimental import pallas as pl
from jax.experimental.pallas import tpu as pltpu
from jax.sharding import PartitionSpec as P

STEPS = 2


highest = lax.Precision.HIGHEST
MESH_ID = pl.DeviceIdType.MESH


def passed_along(value, axis, steps):
    count = lax.axis_size(axis)
    pairs = [(source, (source + steps) % count) for source in range(count)]
    return lax.ppermute(value, axis, pairs)


def padded_2(array, sides, width):
    for axis, dim in sides:
        peers, length = (lax.axis_size(axis), array.shape[dim])
        up = [(i, (i + 1) % peers) for i in range(peers)]
        down = [(j, i) for i, j in up]
        last = lax.slice_in_dim(array, length - width, length, axis=dim)
        leading = lax.slice_in_dim(array, 0, width, axis=dim)
        before = lax.ppermute(last, axis, up)
        after = lax.ppermute(leading, axis, down)
        array = jnp.concatenate([before, array, after], axis=dim)
    return array


def exchange_kernel(axes, sizes, x_ref, o_ref, send_sem, recv_sem, local_sem):
    count = x_ref.shape[0]

    def place(index):
        coords = {}
        for axis, size in reversed(list(zip(axes, sizes))):
            coords[axis] = index % size
            index = index // size
        return coords

    me = 0
    for axis, size in zip(axes, sizes):
        me = me * size + lax.axis_index(axis)
    barrier = pltpu.get_barrier_semaphore()
    for step in range(1, count):
        pl.semaphore_signal(
            barrier, inc=1, device_id=place((me + step) % count), device_id_type=MESH_ID
        )
    pl.semaphore_wait(barrier, count - 1)
    copies = []
    for step in range(1, count):
        hop = (step + 1) // 2 if step % 2 else count - step // 2
        peer = (me + hop) % count
        copy = pltpu.make_async_remote_copy(
            src_ref=x_ref.at[peer],
            dst_ref=o_ref.at[me],
            send_sem=send_sem.at[step - 1],
            recv_sem=recv_sem.at[step - 1],
            device_id=place(peer),
            device_id_type=MESH_ID,
        )
        copy.start()
        copies.append(copy)
    local = pltpu.make_async_copy(x_ref.at[me], o_ref.at[me], local_sem)
    local.start()
    local.wait()
    for copy in copies:
        copy.wait()


def exchange(x, axes, collective_id):
    count = x.shape[0]
    sizes = tuple(lax.axis_size(axis) for axis in axes)
    return pl.pallas_call(
        functools.partial(exchange_kernel, axes, sizes),
        out_shape=jax.ShapeDtypeStruct(x.shape, x.dtype),
        in_specs=[pl.BlockSpec(memory_space=pl.ANY)],
        out_specs=pl.BlockSpec(memory_space=pl.ANY),
        scratch_shapes=[
            pltpu.SemaphoreType.DMA((count - 1,)),
            pltpu.SemaphoreType.DMA((count - 1,)),
            pltpu.SemaphoreType.DMA,
        ],
        compiler_params=pltpu.CompilerParams(
            collective_id=collective_id, has_side_effects=True
        ),
    )(x)


def mode_classes(ax_count, local_modes, classes):
    assert local_modes == 6 and classes == 8 and ax_count % 4 == 0
    slots = np.zeros((4, classes), np.int32)
    for d in range(4):
        given = [c for c in range(classes) if c // 2 != d]
        for index, c in enumerate(given):
            slots[d][c] = index
    class_modes = []
    for c in range(classes):
        modes = []
        for quad in range(ax_count // 4):
            for d in range(4):
                if d != c // 2:
                    modes.append((4 * quad + d) * local_modes + slots[d][c])
        class_modes.append(modes)
    class_modes = np.array(class_modes, np.int32)
    assert sorted(class_modes.reshape(-1).tolist()) == list(range(ax_count * local_modes))
    columns = np.stack([2 * class_modes, 2 * class_modes + 1], axis=-1).reshape(-1)
    return slots, columns


def fourier_tables(columns, kept_modes, order):
    modes_total = columns // 2
    row_index = jnp.asarray(order)[:, None]
    point_index = lax.broadcasted_iota(jnp.int32, (columns, columns), 1)
    mode_index = row_index // 2
    phase = (mode_index * point_index % columns).astype(jnp.float32) * (2.0 * math.pi / columns)
    even_rows = row_index % 2 == 0
    cosine = jnp.cos(phase)
    sine = jnp.sin(phase)
    root = math.sqrt(modes_total)
    synthesis = jnp.where(even_rows, cosine, sine) / root
    weights = jnp.where(mode_index == 0, 1.0, 2.0)
    analysis = jnp.where(even_rows, weights * cosine, 2.0 * sine) * (root / columns)
    analysis = jnp.where(mode_index < kept_modes, analysis, 0.0)
    return (synthesis, analysis)


def body(start_states, radial_inverse, offsets, mode_count):
    groups, components, axial_rows, radial_rows, columns = start_states.shape
    local_modes = radial_inverse.shape[0]
    ax_count = lax.axis_size("ax")
    seg_count = lax.axis_size("seg")
    rad_count = lax.axis_size("rad")
    classes = seg_count * rad_count
    radial_total = radial_rows * rad_count
    class_modes = columns // 2 // classes
    vectors = groups * components * axial_rows
    lanes = vectors * radial_rows
    slots, order = mode_classes(ax_count, local_modes, classes)
    ring = ("seg", "rad")

    me = lax.axis_index("seg") * rad_count + lax.axis_index("rad")
    own = jnp.asarray(slots)[lax.axis_index("ax") % 4, me]
    contribution = lax.dynamic_slice_in_dim(radial_inverse, own, 1, axis=0)
    contribution = jnp.transpose(contribution, (0, 2, 1))
    gathered = lax.all_gather(contribution, "ax", axis=0, tiled=True)
    gathered = gathered.reshape(ax_count // 4, 4, radial_total, radial_total)
    slot = lax.broadcasted_iota(jnp.int32, (1, 3, 1, 1), 1)
    operators = jnp.where(slot < me // 2, gathered[:, 0:3], gathered[:, 1:4])
    operators = operators.reshape(class_modes, radial_total, radial_total)

    natural = np.arange(columns, dtype=np.int32)
    synthesis_first, _ = fourier_tables(columns, mode_count[0], natural)
    synthesis, analysis = fourier_tables(columns, mode_count[0], order)
    radius = (
        (lax.axis_index("rad") * radial_rows + jnp.arange(radial_rows)).astype(jnp.float32) + 0.5
    ) / radial_total
    profile = (1.0 - radius * radius).reshape(1, 1, 1, radial_rows, 1)
    following = passed_along(start_states[0], "seg", -1)
    current = start_states.reshape(lanes, columns)
    for step_index in range(STEPS):
        if step_index == 0:
            physical = jnp.dot(current, synthesis_first, precision=highest)
        else:
            physical = jnp.einsum("jn,jp->np", current, synthesis, precision=highest)
        physical = physical.reshape(groups, components, axial_rows, radial_rows, columns)
        padded = padded_2(physical, (("ax", 2),), 1)
        gradient = (padded[:, :, 2:] - padded[:, :, :-2]) * 20.0
        advecting = profile + padded[:, 2:3, 1:-1]
        forcing = physical - 0.02 * advecting * gradient
        forcing = forcing.reshape(lanes, columns)
        spectral = jnp.einsum("np,jp->jn", forcing, analysis, precision=highest)
        spectral = spectral.reshape(classes, 2 * class_modes, lanes)
        pencils = exchange(spectral, ring, 0)
        pencils = pencils.reshape(
            seg_count, rad_count, class_modes, 2 * vectors, radial_rows
        )
        blocks = operators.reshape(class_modes, rad_count, radial_rows, radial_total)
        solved = sum(
            jnp.einsum(
                "gmns,msr->gmnr", pencils[:, q], blocks[:, q], precision=highest
            )
            for q in range(rad_count)
        )
        solved = solved.reshape(seg_count, class_modes, 2 * vectors, rad_count, radial_rows)
        solved = jnp.transpose(solved, (0, 3, 1, 2, 4)).reshape(classes, 2 * class_modes, lanes)
        returned = exchange(solved, ring, 0)
        current = returned.reshape(columns, lanes)

    chunk = columns // ax_count
    dense = (ax_count, chunk * lanes // 128, 128)
    blocks = exchange(current.reshape(dense), ("ax",), 1)
    blocks = blocks.reshape(ax_count, chunk, groups, components, axial_rows, radial_rows)
    blocks = jnp.transpose(blocks, (1, 2, 3, 0, 4, 5)).reshape(
        chunk, groups, components, ax_count * axial_rows, radial_rows
    )
    shifted = [jnp.roll(blocks[:, member], offsets[member], axis=2) for member in range(groups)]
    blocks = jnp.stack(shifted, axis=1).reshape(
        chunk, groups, components, ax_count, axial_rows, radial_rows
    )
    blocks = jnp.transpose(blocks, (3, 0, 1, 2, 4, 5)).reshape(dense)
    ending = exchange(blocks, ("ax",), 1).reshape(columns, lanes)

    reorder = (jnp.asarray(order)[:, None] == lax.broadcasted_iota(jnp.int32, (columns, columns), 1))
    ending = jnp.einsum("jn,jp->np", ending, reorder.astype(jnp.float32), precision=highest)
    ending = ending.reshape(groups, components, axial_rows, radial_rows, columns)
    upcoming = jnp.concatenate([start_states[1:], following[None]], axis=0)
    return ending - upcoming


def solution(mesh):
    placed = (P("seg", None, "ax", "rad", None), P("ax", None, None), P("seg"), P())
    return jax.shard_map(
        body,
        mesh=mesh,
        in_specs=placed,
        out_specs=P("seg", None, "ax", "rad", None),
        check_vma=False,
    )
```

```python
import functools
import math

import numpy as np
import jax
import jax.numpy as jnp
from jax import lax
from jax.experimental import pallas as pl
from jax.experimental.pallas import tpu as pltpu
from jax.sharding import PartitionSpec as P

STEPS = 2


highest = lax.Precision.HIGHEST
MESH_ID = pl.DeviceIdType.MESH


def passed_along(value, axis, steps):
    count = lax.axis_size(axis)
    pairs = [(source, (source + steps) % count) for source in range(count)]
    return lax.ppermute(value, axis, pairs)


def padded_2(array, sides, width):
    for axis, dim in sides:
        peers, length = (lax.axis_size(axis), array.shape[dim])
        up = [(i, (i + 1) % peers) for i in range(peers)]
        down = [(j, i) for i, j in up]
        last = lax.slice_in_dim(array, length - width, length, axis=dim)
        leading = lax.slice_in_dim(array, 0, width, axis=dim)
        before = lax.ppermute(last, axis, up)
        after = lax.ppermute(leading, axis, down)
        array = jnp.concatenate([before, array, after], axis=dim)
    return array


def exchange_kernel(axes, sizes, x_ref, o_ref, send_sem, recv_sem, local_sem):
    count = x_ref.shape[0]

    def place(index):
        coords = {}
        for axis, size in reversed(list(zip(axes, sizes))):
            coords[axis] = index % size
            index = index // size
        return coords

    me = 0
    for axis, size in zip(axes, sizes):
        me = me * size + lax.axis_index(axis)
    barrier = pltpu.get_barrier_semaphore()
    for step in range(1, count):
        pl.semaphore_signal(
            barrier, inc=1, device_id=place((me + step) % count), device_id_type=MESH_ID
        )
    pl.semaphore_wait(barrier, count - 1)
    copies = []
    for step in range(1, count):
        hop = (step + 1) // 2 if step % 2 else count - step // 2
        peer = (me + hop) % count
        copy = pltpu.make_async_remote_copy(
            src_ref=x_ref.at[peer],
            dst_ref=o_ref.at[me],
            send_sem=send_sem.at[step - 1],
            recv_sem=recv_sem.at[step - 1],
            device_id=place(peer),
            device_id_type=MESH_ID,
        )
        copy.start()
        copies.append(copy)
    local = pltpu.make_async_copy(x_ref.at[me], o_ref.at[me], local_sem)
    local.start()
    local.wait()
    for copy in copies:
        copy.wait()


def exchange(x, axes, collective_id):
    count = x.shape[0]
    sizes = tuple(lax.axis_size(axis) for axis in axes)
    return pl.pallas_call(
        functools.partial(exchange_kernel, axes, sizes),
        out_shape=jax.ShapeDtypeStruct(x.shape, x.dtype),
        in_specs=[pl.BlockSpec(memory_space=pl.ANY)],
        out_specs=pl.BlockSpec(memory_space=pl.ANY),
        scratch_shapes=[
            pltpu.SemaphoreType.DMA((count - 1,)),
            pltpu.SemaphoreType.DMA((count - 1,)),
            pltpu.SemaphoreType.DMA,
        ],
        compiler_params=pltpu.CompilerParams(
            collective_id=collective_id, has_side_effects=True
        ),
    )(x)


def mode_classes(ax_count, local_modes, classes):
    assert local_modes == 6 and classes == 8 and ax_count % 4 == 0
    slots = np.zeros((4, classes), np.int32)
    for d in range(4):
        given = [c for c in range(classes) if c // 2 != d]
        for index, c in enumerate(given):
            slots[d][c] = index
    class_modes = []
    for c in range(classes):
        modes = []
        for quad in range(ax_count // 4):
            for d in range(4):
                if d != c // 2:
                    modes.append((4 * quad + d) * local_modes + slots[d][c])
        class_modes.append(modes)
    class_modes = np.array(class_modes, np.int32)
    assert sorted(class_modes.reshape(-1).tolist()) == list(range(ax_count * local_modes))
    columns = np.stack([2 * class_modes, 2 * class_modes + 1], axis=-1).reshape(-1)
    return slots, columns


def fourier_tables(columns, kept_modes, order):
    modes_total = columns // 2
    row_index = jnp.asarray(order)[:, None]
    point_index = lax.broadcasted_iota(jnp.int32, (columns, columns), 1)
    mode_index = row_index // 2
    phase = (mode_index * point_index % columns).astype(jnp.float32) * (2.0 * math.pi / columns)
    even_rows = row_index % 2 == 0
    cosine = jnp.cos(phase)
    sine = jnp.sin(phase)
    root = math.sqrt(modes_total)
    synthesis = jnp.where(even_rows, cosine, sine) / root
    weights = jnp.where(mode_index == 0, 1.0, 2.0)
    analysis = jnp.where(even_rows, weights * cosine, 2.0 * sine) * (root / columns)
    analysis = jnp.where(mode_index < kept_modes, analysis, 0.0)
    return (synthesis, analysis)


def body(start_states, radial_inverse, offsets, mode_count):
    groups, components, axial_rows, radial_rows, columns = start_states.shape
    local_modes = radial_inverse.shape[0]
    ax_count = lax.axis_size("ax")
    seg_count = lax.axis_size("seg")
    rad_count = lax.axis_size("rad")
    classes = seg_count * rad_count
    radial_total = radial_rows * rad_count
    class_modes = columns // 2 // classes
    vectors = groups * components * axial_rows
    lanes = vectors * radial_rows
    slots, order = mode_classes(ax_count, local_modes, classes)
    ring = ("seg", "rad")

    me = lax.axis_index("seg") * rad_count + lax.axis_index("rad")
    own = jnp.asarray(slots)[lax.axis_index("ax") % 4, me]
    contribution = lax.dynamic_slice_in_dim(radial_inverse, own, 1, axis=0)
    contribution = jnp.transpose(contribution, (0, 2, 1))
    gathered = lax.all_gather(contribution, "ax", axis=0, tiled=True)
    gathered = gathered.reshape(ax_count // 4, 4, radial_total, radial_total)
    slot = lax.broadcasted_iota(jnp.int32, (1, 3, 1, 1), 1)
    operators = jnp.where(slot < me // 2, gathered[:, 0:3], gathered[:, 1:4])
    operators = operators.reshape(class_modes, radial_total, radial_total)

    natural = np.arange(columns, dtype=np.int32)
    synthesis_first, _ = fourier_tables(columns, mode_count[0], natural)
    synthesis, analysis = fourier_tables(columns, mode_count[0], order)
    radius = (
        (lax.axis_index("rad") * radial_rows + jnp.arange(radial_rows)).astype(jnp.float32) + 0.5
    ) / radial_total
    profile = (1.0 - radius * radius).reshape(1, 1, 1, radial_rows, 1)
    following = passed_along(start_states[0], "seg", -1)
    current = start_states.reshape(lanes, columns)
    for step_index in range(STEPS):
        if step_index == 0:
            physical = jnp.dot(current, synthesis_first, precision=highest)
        else:
            physical = jnp.einsum("jn,jp->np", current, synthesis, precision=highest)
        physical = physical.reshape(groups, components, axial_rows, radial_rows, columns)
        padded = padded_2(physical, (("ax", 2),), 1)
        gradient = (padded[:, :, 2:] - padded[:, :, :-2]) * 20.0
        advecting = profile + padded[:, 2:3, 1:-1]
        forcing = physical - 0.02 * advecting * gradient
        forcing = forcing.reshape(lanes, columns)
        spectral = jnp.einsum("np,jp->jn", forcing, analysis, precision=highest)
        spectral = spectral.reshape(classes, 2 * class_modes, lanes)
        pencils = exchange(spectral, ring, 0)
        pencils = pencils.reshape(
            seg_count, rad_count, class_modes, 2 * vectors, radial_rows
        )
        blocks = operators.reshape(class_modes, rad_count, radial_rows, radial_total)
        solved = sum(
            jnp.einsum(
                "gmns,msr->gmnr", pencils[:, q], blocks[:, q], precision=highest
            )
            for q in range(rad_count)
        )
        solved = solved.reshape(seg_count, class_modes, 2 * vectors, rad_count, radial_rows)
        solved = jnp.transpose(solved, (0, 3, 1, 2, 4)).reshape(classes, 2 * class_modes, lanes)
        returned = exchange(solved, ring, 0)
        current = returned.reshape(columns, lanes)

    chunk = columns // ax_count
    dense = (ax_count, chunk * lanes // 128, 128)
    blocks = exchange(current.reshape(dense), ("ax",), 1)
    plane = axial_rows * radial_rows
    blocks = blocks.reshape(ax_count, chunk, groups, components, plane)
    within = lax.broadcasted_iota(jnp.int32, (1, 1, 1, plane), 3) // radial_rows
    shifted = []
    for member in range(groups):
        whole, part = offsets[member] // axial_rows, offsets[member] % axial_rows
        source = blocks[:, :, member]
        near = jnp.roll(jnp.roll(source, whole, axis=0), part * radial_rows, axis=3)
        far = jnp.roll(jnp.roll(source, whole + 1, axis=0), part * radial_rows, axis=3)
        shifted.append(jnp.where(within >= part, near, far))
    blocks = jnp.stack(shifted, axis=2).reshape(dense)
    ending = exchange(blocks, ("ax",), 1).reshape(columns, lanes)

    reorder = (jnp.asarray(order)[:, None] == lax.broadcasted_iota(jnp.int32, (columns, columns), 1))
    ending = jnp.einsum("jn,jp->np", ending, reorder.astype(jnp.float32), precision=highest)
    ending = ending.reshape(groups, components, axial_rows, radial_rows, columns)
    upcoming = jnp.concatenate([start_states[1:], following[None]], axis=0)
    return ending - upcoming


def solution(mesh):
    placed = (P("seg", None, "ax", "rad", None), P("ax", None, None), P("seg"), P())
    return jax.shard_map(
        body,
        mesh=mesh,
        in_specs=placed,
        out_specs=P("seg", None, "ax", "rad", None),
        check_vma=False,
    )
```

```python
import functools
import math

import numpy as np
import jax
import jax.numpy as jnp
from jax import lax
from jax.experimental import pallas as pl
from jax.experimental.pallas import tpu as pltpu
from jax.sharding import PartitionSpec as P

STEPS = 2


highest = lax.Precision.HIGHEST
MESH_ID = pl.DeviceIdType.MESH


def passed_along(value, axis, steps):
    count = lax.axis_size(axis)
    pairs = [(source, (source + steps) % count) for source in range(count)]
    return lax.ppermute(value, axis, pairs)


def padded_2(array, sides, width):
    for axis, dim in sides:
        peers, length = (lax.axis_size(axis), array.shape[dim])
        up = [(i, (i + 1) % peers) for i in range(peers)]
        down = [(j, i) for i, j in up]
        last = lax.slice_in_dim(array, length - width, length, axis=dim)
        leading = lax.slice_in_dim(array, 0, width, axis=dim)
        before = lax.ppermute(last, axis, up)
        after = lax.ppermute(leading, axis, down)
        array = jnp.concatenate([before, array, after], axis=dim)
    return array


def exchange_kernel(axes, sizes, x_ref, o_ref, send_sem, recv_sem, local_sem):
    count = x_ref.shape[0]

    def place(index):
        coords = {}
        for axis, size in reversed(list(zip(axes, sizes))):
            coords[axis] = index % size
            index = index // size
        return coords

    me = 0
    for axis, size in zip(axes, sizes):
        me = me * size + lax.axis_index(axis)
    barrier = pltpu.get_barrier_semaphore()
    for step in range(1, count):
        pl.semaphore_signal(
            barrier, inc=1, device_id=place((me + step) % count), device_id_type=MESH_ID
        )
    pl.semaphore_wait(barrier, count - 1)
    copies = []
    for step in range(1, count):
        hop = (step + 1) // 2 if step % 2 else count - step // 2
        peer = (me + hop) % count
        copy = pltpu.make_async_remote_copy(
            src_ref=x_ref.at[peer],
            dst_ref=o_ref.at[me],
            send_sem=send_sem.at[step - 1],
            recv_sem=recv_sem.at[step - 1],
            device_id=place(peer),
            device_id_type=MESH_ID,
        )
        copy.start()
        copies.append(copy)
    local = pltpu.make_async_copy(x_ref.at[me], o_ref.at[me], local_sem)
    local.start()
    local.wait()
    for copy in copies:
        copy.wait()


def exchange(x, axes, collective_id):
    count = x.shape[0]
    sizes = tuple(lax.axis_size(axis) for axis in axes)
    return pl.pallas_call(
        functools.partial(exchange_kernel, axes, sizes),
        out_shape=jax.ShapeDtypeStruct(x.shape, x.dtype),
        in_specs=[pl.BlockSpec(memory_space=pl.ANY)],
        out_specs=pl.BlockSpec(memory_space=pl.ANY),
        scratch_shapes=[
            pltpu.SemaphoreType.DMA((count - 1,)),
            pltpu.SemaphoreType.DMA((count - 1,)),
            pltpu.SemaphoreType.DMA,
        ],
        compiler_params=pltpu.CompilerParams(
            collective_id=collective_id, has_side_effects=True
        ),
    )(x)


def mode_classes(ax_count, local_modes, classes):
    assert local_modes == 6 and classes == 8 and ax_count % 4 == 0
    slots = np.zeros((4, classes), np.int32)
    for d in range(4):
        given = [c for c in range(classes) if c // 2 != d]
        for index, c in enumerate(given):
            slots[d][c] = index
    class_modes = []
    for c in range(classes):
        modes = []
        for quad in range(ax_count // 4):
            for d in range(4):
                if d != c // 2:
                    modes.append((4 * quad + d) * local_modes + slots[d][c])
        class_modes.append(modes)
    class_modes = np.array(class_modes, np.int32)
    assert sorted(class_modes.reshape(-1).tolist()) == list(range(ax_count * local_modes))
    columns = np.stack([2 * class_modes, 2 * class_modes + 1], axis=-1).reshape(-1)
    return slots, columns


def fourier_tables(columns, kept_modes, order):
    modes_total = columns // 2
    row_index = jnp.asarray(order)[:, None]
    point_index = lax.broadcasted_iota(jnp.int32, (columns, columns), 1)
    mode_index = row_index // 2
    phase = (mode_index * point_index % columns).astype(jnp.float32) * (2.0 * math.pi / columns)
    even_rows = row_index % 2 == 0
    cosine = jnp.cos(phase)
    sine = jnp.sin(phase)
    root = math.sqrt(modes_total)
    synthesis = jnp.where(even_rows, cosine, sine) / root
    weights = jnp.where(mode_index == 0, 1.0, 2.0)
    analysis = jnp.where(even_rows, weights * cosine, 2.0 * sine) * (root / columns)
    analysis = jnp.where(mode_index < kept_modes, analysis, 0.0)
    return (synthesis, analysis)


def body(start_states, radial_inverse, offsets, mode_count):
    groups, components, axial_rows, radial_rows, columns = start_states.shape
    local_modes = radial_inverse.shape[0]
    ax_count = lax.axis_size("ax")
    seg_count = lax.axis_size("seg")
    rad_count = lax.axis_size("rad")
    classes = seg_count * rad_count
    radial_total = radial_rows * rad_count
    class_modes = columns // 2 // classes
    vectors = groups * components * axial_rows
    lanes = vectors * radial_rows
    slots, order = mode_classes(ax_count, local_modes, classes)
    ring = ("seg", "rad")

    me = lax.axis_index("seg") * rad_count + lax.axis_index("rad")
    own = jnp.asarray(slots)[lax.axis_index("ax") % 4, me]
    contribution = lax.dynamic_slice_in_dim(radial_inverse, own, 1, axis=0)
    contribution = jnp.transpose(contribution, (0, 2, 1))
    gathered = lax.all_gather(contribution, "ax", axis=0, tiled=True)
    gathered = gathered.reshape(ax_count // 4, 4, radial_total, radial_total)
    operators = jnp.concatenate(
        [
            lax.dynamic_slice_in_dim(gathered, u + (u >= me // 2).astype(jnp.int32), 1, axis=1)
            for u in range(3)
        ],
        axis=1,
    )
    operators = operators.reshape(class_modes, radial_total, radial_total)

    natural = np.arange(columns, dtype=np.int32)
    synthesis_first, _ = fourier_tables(columns, mode_count[0], natural)
    synthesis, analysis = fourier_tables(columns, mode_count[0], order)
    radius = (
        (lax.axis_index("rad") * radial_rows + jnp.arange(radial_rows)).astype(jnp.float32) + 0.5
    ) / radial_total
    profile = (1.0 - radius * radius).reshape(1, 1, 1, radial_rows, 1)
    following = passed_along(start_states[0], "seg", -1)
    current = start_states.reshape(lanes, columns)
    for step_index in range(STEPS):
        if step_index == 0:
            physical = jnp.dot(current, synthesis_first, precision=highest)
        else:
            physical = jnp.einsum("jn,jp->np", current, synthesis, precision=highest)
        physical = physical.reshape(groups, components, axial_rows, radial_rows, columns)
        padded = padded_2(physical, (("ax", 2),), 1)
        gradient = (padded[:, :, 2:] - padded[:, :, :-2]) * 20.0
        advecting = profile + padded[:, 2:3, 1:-1]
        forcing = physical - 0.02 * advecting * gradient
        forcing = forcing.reshape(lanes, columns)
        spectral = jnp.einsum("np,jp->jn", forcing, analysis, precision=highest)
        spectral = spectral.reshape(classes, 2 * class_modes, lanes)
        pencils = exchange(spectral, ring, 0)
        pencils = pencils.reshape(
            seg_count, rad_count, class_modes, 2 * vectors, radial_rows
        )
        blocks = operators.reshape(class_modes, rad_count, radial_rows, radial_total)
        solved = sum(
            jnp.einsum(
                "gmns,msr->gmnr", pencils[:, q], blocks[:, q], precision=highest
            )
            for q in range(rad_count)
        )
        solved = solved.reshape(seg_count, class_modes, 2 * vectors, rad_count, radial_rows)
        solved = jnp.transpose(solved, (0, 3, 1, 2, 4)).reshape(classes, 2 * class_modes, lanes)
        returned = exchange(solved, ring, 0)
        current = returned.reshape(columns, lanes)

    chunk = columns // ax_count
    dense = (ax_count, chunk * lanes // 128, 128)
    blocks = exchange(current.reshape(dense), ("ax",), 1)
    blocks = blocks.reshape(ax_count, chunk, groups, components, axial_rows, radial_rows)
    blocks = jnp.transpose(blocks, (1, 2, 3, 0, 4, 5)).reshape(
        chunk, groups, components, ax_count * axial_rows, radial_rows
    )
    shifted = [jnp.roll(blocks[:, member], offsets[member], axis=2) for member in range(groups)]
    blocks = jnp.stack(shifted, axis=1).reshape(
        chunk, groups, components, ax_count, axial_rows, radial_rows
    )
    blocks = jnp.transpose(blocks, (3, 0, 1, 2, 4, 5)).reshape(dense)
    ending = exchange(blocks, ("ax",), 1).reshape(columns, lanes)

    reorder = (jnp.asarray(order)[:, None] == lax.broadcasted_iota(jnp.int32, (columns, columns), 1))
    ending = jnp.einsum("jn,jp->np", ending, reorder.astype(jnp.float32), precision=highest)
    ending = ending.reshape(groups, components, axial_rows, radial_rows, columns)
    upcoming = jnp.concatenate([start_states[1:], following[None]], axis=0)
    return ending - upcoming


def solution(mesh):
    placed = (P("seg", None, "ax", "rad", None), P("ax", None, None), P("seg"), P())
    return jax.shard_map(
        body,
        mesh=mesh,
        in_specs=placed,
        out_specs=P("seg", None, "ax", "rad", None),
        check_vma=False,
    )
```
